32 devices in a mesh: lon: 8 (over y, x, core), sub: 4 (over z).
Axes of the slice: x: 2, y: 2, z: 4, core: 2. Of those that a mesh axis runs over, the one named last changes fastest.
Arguments:
- atm_tracer: float32 [128, 128, 2048], P('sub', None, 'lon'), may hold values from -6 to 6
- courant: float32 [128, 128, 2048], P('sub', None, 'lon'), may hold values from -0.9 to 0.9
- column_inverse: float32 [8, 128, 128], replicated
- heat_exchange_factor: float32 [128, 2048], P(None, 'lon'), may hold values from 0.3 to 3
- ocean_temp: float32 [32, 32, 1024], P(None, 'sub', 'lon'), may hold values from -6 to 6
- diffusivity: float32 [32, 1024], P('sub', 'lon'), may hold values from 0.04 to 0.2
- ocean_inverse: float32 [32, 32], replicated
- land_mask: int32 [32, 1024], P('sub', 'lon'), may hold values 0 or 1
- regrid_weight_blocks: float32 [64, 128, 128], replicated, may hold values from -0.25 to 0.25
- a2o_src: int32 [32, 8, 4], P('sub', 'lon'), may hold values from 0 to 2047, as said below
- a2o_wgt: int32 [32, 8, 4], P('sub', 'lon'), may hold values from 0 to 63
- ocean_to_atmos_source: int32 [128, 16, 4], P(None, 'lon'), may hold values from 0 to 255, as said below
- ocean_to_atmos_weight: int32 [128, 16, 4], P(None, 'lon'), may hold values from 0 to 63
Outputs:
- atmos_temp_updated: float32 [128, 128, 2048], P('sub', None, 'lon')
- ocean_new: float32 [32, 32, 1024], P(None, 'sub', 'lon')
- atmos_heat_flux: float32 [128, 2048], P('sub', 'lon')
The draws below stay inside these ranges and needn't reach their ends.
Inputs may be any that keep to these rules, and one draw needn't show every extreme that they name: `a2o_src`: for ocean block row r in tile column t, every entry names an atmosphere block of a row in r // 8 * 32 to (r // 8 + 1) * 32 - 1 and of a column group g with (g - t * 2) mod 16 below 4. `ocean_to_atmos_source`: for atmosphere block row r and column group g, every entry names an ocean block of a row in r // 32 * 8 to (r // 32 + 1) * 8 - 1 and of tile column s or s - 1 (mod 8), where s = g // 2.
All inputs are finite; a program needn't handle non-finite values. No bound on the sum of `land_mask` on one device may be relied on, other than what follows from the above.
Results may differ from the reference program's by a relative error of at most 0.000096.
Values sent between devices are 32-bit elements; how exact they have to be, the bound alone decides.
A program may use at most 64 MiB of HBM per device.

```python
import math
import jax
import jax.numpy as jnp
from jax import lax

ATMOS_LEVELS = 128
ATMOS_LAT_ROWS = 128
ALON_DEV = 256
OLON_DEV = 128
OLAT_DEV = 8
OLEV = 32
NBAND = 8
INTERSECT_COUNT = 4
NW = 64
TILES = 8
ATMOS_LON_CELLS = 2048
OLAT = 32
OLON = 1024
NG = 16
ABAND = 32


def square_inverse(key, count, order):
    key_diag, key_off = jax.random.split(key, 2)
    diag = jax.random.uniform(key_diag, (count, order), minval=0.6, maxval=1.4)
    offdiag = jax.random.normal(key_off, (count, order, order)) * (0.5 / math.sqrt(order))
    matrix = offdiag + diag[:, :, None] * jnp.eye(order, dtype=jnp.float32)[None]
    return matrix.astype(jnp.float32)


def draw_column_inverse(key, part):
    return square_inverse(jax.random.fold_in(key, 11), NBAND, ATMOS_LEVELS)


def draw_ocean_inverse(key, part):
    return square_inverse(jax.random.fold_in(key, 12), 1, OLEV)[0]


def draw_a2o_src(key, part):
    key_row, key_grp = jax.random.split(jax.random.fold_in(key, 21))
    groups = ALON_DEV // OLON_DEV
    rows = jnp.arange(OLAT, dtype=jnp.int32)[:, None, None]
    tiles = jnp.arange(TILES, dtype=jnp.int32)[None, :, None]
    atm_row = rows // OLAT_DEV * ABAND + jax.random.randint(key_row, (OLAT, TILES, INTERSECT_COUNT), 0, ABAND)
    atm_grp = (tiles * groups + jax.random.randint(key_grp, (OLAT, TILES, INTERSECT_COUNT), 0, 2 * groups)) % NG
    return (atm_row * NG + atm_grp).astype(jnp.int32)


def draw_ocean_to_atmos_source(key, part):
    key_row, key_tile = jax.random.split(jax.random.fold_in(key, 31))
    groups = ALON_DEV // OLON_DEV
    rows = jnp.arange(ATMOS_LAT_ROWS, dtype=jnp.int32)[:, None, None]
    grps = jnp.arange(NG, dtype=jnp.int32)[None, :, None]
    ocean_row = rows // ABAND * OLAT_DEV + jax.random.randint(key_row, (ATMOS_LAT_ROWS, NG, INTERSECT_COUNT), 0, OLAT_DEV)
    ocean_tile = (grps // groups - jax.random.randint(key_tile, (ATMOS_LAT_ROWS, NG, INTERSECT_COUNT), 0, 2)) % TILES
    return (ocean_row * TILES + ocean_tile).astype(jnp.int32)


def with_ends(values, stream_key, least, high):
    index_at = [jax.random.randint(jax.random.fold_in(stream_key, axis), (), 0, length) for axis, length in enumerate(values.shape)]
    main_axis = values.shape.index(max(values.shape))
    next_to = index_at[:main_axis] + [(index_at[main_axis] + 1) % values.shape[main_axis]] + index_at[main_axis + 1:]
    return values.at[tuple(index_at)].set(least).at[tuple(next_to)].set(high)


def block_levels(stream_key, shape, cuts, least, top_value):
    def one(position, blocks):
        heights = jax.random.uniform(jax.random.fold_in(jax.random.fold_in(stream_key, 6), position), (blocks,), jnp.float32, least / len(cuts), top_value / len(cuts))
        return jnp.repeat(jnp.exp(heights), shape[position] // blocks).reshape((-1,) + (1,) * (len(shape) - position - 1))

    loudness = one(*cuts[0])
    for cut in cuts[1:]:
        loudness = loudness * one(*cut)
    return loudness


def scatter_about(own_key, extent, scale, reach, cuts=(), kind=jnp.bfloat16):
    drawn = scale * jax.random.normal(own_key, extent, jnp.float32)
    if cuts:
        drawn = drawn * block_levels(own_key, extent, cuts, -0.22, 0.18)
    return jnp.clip(drawn, -reach, reach).astype(kind)


def setup_inputs(seed: int = 0) -> dict:
    keys = jax.random.split(jax.random.key(seed), 14)
    return {
        "atm_tracer": scatter_about(keys[0], (ATMOS_LEVELS, ATMOS_LAT_ROWS, ATMOS_LON_CELLS), 1.0, 6.0, ((0, 4), (2, 8)), jnp.float32),
        "courant": jnp.clip(jax.random.uniform(keys[1], (ATMOS_LEVELS, ATMOS_LAT_ROWS, ATMOS_LON_CELLS), jnp.float32, -0.9, 0.9) * block_levels(keys[1], (ATMOS_LEVELS, ATMOS_LAT_ROWS, ATMOS_LON_CELLS), ((0, 4), (2, 8)), -0.4, 0.0), -0.9, 0.9),
        "column_inverse": draw_column_inverse(jax.random.fold_in(keys[13], 71), 0),
        "heat_exchange_factor": jnp.clip(jnp.exp(math.log(3.0) - 2.3025851 * jax.random.uniform(keys[3], (ATMOS_LAT_ROWS, ATMOS_LON_CELLS), jnp.float32) ** block_levels(keys[3], (ATMOS_LAT_ROWS, ATMOS_LON_CELLS), ((1, 8),), -0.2, 0.2)), 0.3, 3.0),
        "ocean_temp": scatter_about(keys[4], (OLEV, OLAT, OLON), 1.0, 6.0, ((1, 4), (2, 8)), jnp.float32),
        "diffusivity": jnp.clip(0.04 + 0.16 * jax.random.uniform(keys[5], (OLAT, OLON), jnp.float32) ** block_levels(keys[5], (OLAT, OLON), ((0, 4), (1, 8)), -0.2, 0.2), 0.04, 0.2),
        "ocean_inverse": draw_ocean_inverse(jax.random.fold_in(keys[13], 71), 0),
        "land_mask": with_ends((jax.random.randint(keys[7], (OLAT, OLON), 0, 4) < 3).astype(jnp.int32), jax.random.fold_in(keys[7], 1), 0, 1),
        "regrid_weight_blocks": scatter_about(keys[8], (NW, OLON_DEV, OLON_DEV), (OLON_DEV * INTERSECT_COUNT) ** -0.5, 0.25, (), jnp.float32),
        "a2o_src": draw_a2o_src(jax.random.fold_in(keys[13], 71), 0),
        "a2o_wgt": with_ends(jax.random.randint(keys[10], (OLAT, TILES, INTERSECT_COUNT), 0, NW), jax.random.fold_in(keys[10], 1), 0, NW - 1).astype(jnp.int32),
        "ocean_to_atmos_source": draw_ocean_to_atmos_source(jax.random.fold_in(keys[13], 71), 0),
        "ocean_to_atmos_weight": with_ends(jax.random.randint(keys[12], (ATMOS_LAT_ROWS, NG, INTERSECT_COUNT), 0, NW), jax.random.fold_in(keys[12], 1), 0, NW - 1).astype(jnp.int32),
    }


def regrid_block_list(blocks, src_ids, wgt_ids, weights):
    count = src_ids.shape[0]
    width = src_ids.shape[1]
    step = math.gcd(count, 16)

    def one_group(pair):
        src_part, wgt_part = pair
        picked = blocks[src_part]
        mats = weights[wgt_part]
        return jnp.einsum("dkij,dkj->di", mats, picked, precision=lax.Precision.HIGHEST)

    result = lax.map(one_group, (src_ids.reshape(count // step, step, width), wgt_ids.reshape(count // step, step, width)))
    return result.reshape(count, blocks.shape[1])


def reference(atm_tracer, courant, column_inverse, heat_exchange_factor, ocean_temp, diffusivity, ocean_inverse, land_mask, regrid_weight_blocks, a2o_src, a2o_wgt, ocean_to_atmos_source, ocean_to_atmos_weight):
    west = jnp.roll(atm_tracer, 1, axis=2)
    east = jnp.roll(atm_tracer, -1, axis=2)
    advected = atm_tracer - jnp.maximum(courant, 0.0) * (atm_tracer - west) - jnp.minimum(courant, 0.0) * (east - atm_tracer)
    rows_band = ATMOS_LAT_ROWS // NBAND
    banded = advected.reshape(ATMOS_LEVELS, NBAND, rows_band * ATMOS_LON_CELLS)
    atmos_temp_updated = jnp.einsum("blm,mbc->lbc", column_inverse, banded, precision=lax.Precision.HIGHEST).reshape(ATMOS_LEVELS, ATMOS_LAT_ROWS, ATMOS_LON_CELLS)
    sea_mask = land_mask.astype(jnp.float32)
    sea = sea_mask * ocean_temp[0]
    ocean_block_list = sea.reshape(OLAT * TILES, OLON_DEV)
    sea_surface_temp_atmos = regrid_block_list(ocean_block_list, ocean_to_atmos_source.reshape(-1, INTERSECT_COUNT), ocean_to_atmos_weight.reshape(-1, INTERSECT_COUNT), regrid_weight_blocks).reshape(ATMOS_LAT_ROWS, ATMOS_LON_CELLS)
    atmos_heat_flux = heat_exchange_factor * (sea_surface_temp_atmos - atmos_temp_updated[ATMOS_LEVELS - 1])
    flux_blocks = atmos_heat_flux.reshape(ATMOS_LAT_ROWS * NG, OLON_DEV)
    flux_ocean = regrid_block_list(flux_blocks, a2o_src.reshape(-1, INTERSECT_COUNT), a2o_wgt.reshape(-1, INTERSECT_COUNT), regrid_weight_blocks).reshape(OLAT, OLON)
    temp = ocean_temp
    o_west = jnp.roll(temp, 1, axis=2)
    o_east = jnp.roll(temp, -1, axis=2)
    folded = jnp.flip(temp[:, OLAT - 1, :], axis=1)
    north = jnp.concatenate([temp[:, 1:, :], folded[:, None, :]], axis=1)
    south = jnp.concatenate([temp[:, :1, :], temp[:, :-1, :]], axis=1)
    lap = o_west + o_east + north + south - 4.0 * temp
    stepped = sea_mask * (temp + diffusivity * lap)
    stepped = stepped.at[0].add(sea_mask * flux_ocean)
    ocean_new = jnp.einsum("lm,mc->lc", ocean_inverse, stepped.reshape(OLEV, OLAT * OLON), precision=lax.Precision.HIGHEST).reshape(OLEV, OLAT, OLON)
    return atmos_temp_updated, ocean_new, atmos_heat_flux
```

```python
import functools

import jax
import jax.numpy as jnp
from jax import lax
from jax.experimental import pallas as pl
from jax.experimental.pallas import tpu as pltpu
from jax.sharding import PartitionSpec as P

HI = lax.Precision.HIGHEST
MESH = pl.DeviceIdType.MESH
ROWS = 8
LANES = 128


def dot(a, b):
    return jnp.dot(a, b, precision=HI, preferred_element_type=jnp.float32)


def dot_nt(a, b):
    return lax.dot_general(
        a, b, (((1,), (1,)), ((), ())), precision=HI, preferred_element_type=jnp.float32
    )


def one_hot(ids, count):
    cols = lax.broadcasted_iota(jnp.int32, (ids.shape[0], count), 1)
    return jnp.where(cols == ids, 1.0, 0.0).astype(jnp.float32)


def kernel(
    n_lon,
    n_sub,
    atm_hbm,
    cour_hbm,
    colinv_hbm,
    heat_ref,
    ocean_ref,
    diff_ref,
    oinv_ref,
    mask_ref,
    w_hbm,
    a2o_src_ref,
    a2o_wgt_ref,
    o2a_src_ref,
    o2a_wgt_ref,
    out_ref,
    onew_ref,
    flux_ref,
    xbuf,
    cbuf,
    adv,
    cols,
    res,
    tmp,
    tmp2,
    wbuf,
    inv,
    halo,
    halo_in,
    sea,
    tile_in,
    edge,
    edge_in,
    fluxbuf,
    flux_in,
    picked,
    apicked,
    sst,
    otmp,
    otmp2,
    local_sem,
    own_sem,
    send1,
    recv1,
    send2,
    recv2,
    hsend,
    hrecv,
):
    lon = lax.axis_index("lon")
    sub = lax.axis_index("sub")
    lev_dev, alat, alon = xbuf.shape
    levels = lev_dev * n_sub
    aband = alat // n_sub
    nchunk = aband // ROWS
    local_bands = inv.shape[0]
    rows_band = aband // local_bands
    groups = alon // LANES
    ngroups = groups * n_lon
    olev, orows, _ = ocean_ref.shape
    nw = wbuf.shape[0]
    width = a2o_src_ref.shape[2]

    east = lax.rem(lon + 1, n_lon)
    west = lax.rem(lon + n_lon - 1, n_lon)
    mirror = n_lon - 1 - lon
    north = lax.rem(sub + 1, n_sub)
    south = lax.rem(sub + n_sub - 1, n_sub)

    load_x = pltpu.make_async_copy(atm_hbm, xbuf, local_sem.at[0])
    load_c = pltpu.make_async_copy(cour_hbm, cbuf, local_sem.at[1])
    load_i = pltpu.make_async_copy(
        colinv_hbm.at[pl.ds(sub * local_bands, local_bands)], inv, local_sem.at[2]
    )
    load_w = pltpu.make_async_copy(w_hbm, wbuf, local_sem.at[3])
    load_x.start()
    load_c.start()
    load_i.start()
    load_w.start()

    barrier = pltpu.get_barrier_semaphore()
    for target in (east, west, mirror):
        pl.semaphore_signal(barrier, inc=1, device_id=(target, sub), device_id_type=MESH)
    for off in range(1, n_sub):
        peer = lax.rem(sub + off, n_sub)
        pl.semaphore_signal(barrier, inc=1, device_id=(lon, peer), device_id_type=MESH)
    pl.semaphore_wait(barrier, 3 + n_sub - 1)

    def remote(src, dst, ssem, rsem, target):
        return pltpu.make_async_remote_copy(
            src_ref=src, dst_ref=dst, send_sem=ssem, recv_sem=rsem,
            device_id=target, device_id_type=MESH,
        )

    lane = lax.broadcasted_iota(jnp.int32, (alat, LANES), 1)
    load_x.wait()
    halo[...] = jnp.zeros_like(halo)

    def pack(l, carry):
        tail, head = carry
        t = xbuf[l, :, alon - LANES :]
        h = xbuf[l, :, :LANES]
        tail = jnp.where(lane == l, pltpu.roll(t, lax.rem(l + 1, LANES), 1), tail)
        head = jnp.where(lane == l, pltpu.roll(h, l, 1), head)
        return tail, head

    zero = jnp.zeros((alat, LANES), jnp.float32)
    tail, head = lax.fori_loop(0, lev_dev, pack, (zero, zero), unroll=4)
    halo[0] = tail
    halo[1] = head
    h_east = remote(halo.at[0], halo_in.at[0], hsend.at[0], hrecv.at[0], (east, sub))
    h_west = remote(halo.at[1], halo_in.at[1], hsend.at[1], hrecv.at[1], (west, sub))
    h_east.start()
    h_west.start()

    maskf = mask_ref[...].astype(jnp.float32)
    sea[0] = maskf * ocean_ref[0]
    edge[0] = ocean_ref[:, 0, :]
    edge[1] = ocean_ref[:, orows - 1, :]

    load_c.wait()
    h_east.wait()
    h_west.wait()

    wide = lax.broadcasted_iota(jnp.int32, (ROWS, alon), 1)
    sends1 = []
    owns = []
    for t in range(nchunk):

        def advect(l, carry, t=t):
            for d in range(n_sub):
                rows = slice(d * aband + t * ROWS, d * aband + (t + 1) * ROWS)
                x = xbuf[l, rows, :]
                c = cbuf[l, rows, :]
                hw = pltpu.roll(halo_in[0, rows, :], lax.rem(LANES - l, LANES), 1)
                he = pltpu.roll(halo_in[1, rows, :], LANES - 1 - l, 1)
                edges = jnp.concatenate([hw] * (groups - 1) + [he], axis=1)
                xw = jnp.where(wide == 0, edges, pltpu.roll(x, 1, 1))
                xe = jnp.where(wide == alon - 1, edges, pltpu.roll(x, alon - 1, 1))
                adv[l, rows, :] = (
                    x - jnp.maximum(c, 0.0) * (x - xw) - jnp.minimum(c, 0.0) * (xe - x)
                )
            return carry

        lax.fori_loop(0, lev_dev, advect, 0, unroll=4)
        for off in [n_sub // 2] + [o for o in range(n_sub - 1, 0, -1) if o != n_sub // 2]:
            peer = lax.rem(sub + off, n_sub)
            cp = remote(
                adv.at[:, pl.ds(peer * aband + t * ROWS, ROWS), :],
                cols.at[pl.ds(sub * lev_dev, lev_dev), pl.ds(t * ROWS, ROWS), :],
                send1.at[t, off],
                recv1.at[t, off],
                (lon, peer),
            )
            cp.start()
            sends1.append((t, cp))
        own = pltpu.make_async_copy(
            adv.at[:, pl.ds(sub * aband + t * ROWS, ROWS), :],
            cols.at[pl.ds(sub * lev_dev, lev_dev), pl.ds(t * ROWS, ROWS), :],
            own_sem.at[0, t],
        )
        own.start()
        owns.append(own)
        if t == 0:
            ocean_copies = [
                remote(sea.at[0], sea.at[1], hsend.at[2], hrecv.at[2], (east, sub)),
                remote(ocean_ref, tile_in.at[0], hsend.at[3], hrecv.at[3], (east, sub)),
                remote(ocean_ref, tile_in.at[1], hsend.at[4], hrecv.at[4], (west, sub)),
                remote(edge.at[1], edge_in.at[0], hsend.at[5], hrecv.at[5], (lon, north)),
                remote(edge.at[0], edge_in.at[1], hsend.at[6], hrecv.at[6], (lon, south)),
                remote(edge.at[1], edge_in.at[2], hsend.at[7], hrecv.at[7], (mirror, sub)),
            ]
            for cp in ocean_copies:
                cp.start()

    load_i.wait()
    load_w.wait()
    ocean_copies[0].wait()
    window = jnp.concatenate([sea[1], sea[0]], axis=0)
    band = pl.ds(sub * aband, aband)
    for g in range(groups):
        for k in range(width):
            src = o2a_src_ref[band, g, :][:, k : k + 1]
            tile = jnp.remainder(src % n_lon - lon + 1, n_lon)
            ids = tile * orows + (src // n_lon - sub * orows)
            picked[k, g * aband : (g + 1) * aband, :] = dot(one_hot(ids, 2 * orows), window)
    wg = jnp.concatenate([o2a_wgt_ref[band, g, :] for g in range(groups)], axis=0)

    def sst_step(w, acc):
        part = jnp.where(wg[:, 0:1] == w, picked[0], 0.0)
        for k in range(1, width):
            part = part + jnp.where(wg[:, k : k + 1] == w, picked[k], 0.0)
        return acc + dot_nt(part, wbuf[w])

    acc = lax.fori_loop(
        0, nw, sst_step, jnp.zeros((groups * aband, LANES), jnp.float32), unroll=2
    )
    for g in range(groups):
        sst[:, g * LANES : (g + 1) * LANES] = acc[g * aband : (g + 1) * aband]

    sends2 = []
    for t in range(nchunk):
        for tt, cp in sends1:
            if tt == t:
                cp.wait()
        owns[t].wait()
        rows = slice(t * ROWS, (t + 1) * ROWS)
        band_inv = inv[t * ROWS // rows_band]

        def turn(i, carry, rows=rows):
            part = cols[pl.ds(i * ROWS, ROWS), rows, :]
            tmp[:, pl.ds(i * ROWS, ROWS), :] = jnp.swapaxes(part, 0, 1)
            return carry

        lax.fori_loop(0, levels // ROWS, turn, 0, unroll=2)

        def solve(r, carry, t=t):
            tmp2[r] = dot(inv[t * ROWS // rows_band], tmp[r])
            return carry

        lax.fori_loop(0, ROWS, solve, 0)

        def back(i, carry, rows=rows):
            part = tmp2[:, pl.ds(i * ROWS, ROWS), :]
            res[pl.ds(i * ROWS, ROWS), rows, :] = jnp.swapaxes(part, 0, 1)
            return carry

        lax.fori_loop(0, levels // ROWS, back, 0, unroll=2)
        for off in [n_sub // 2] + [o for o in range(n_sub - 1, 0, -1) if o != n_sub // 2]:
            peer = lax.rem(sub + off, n_sub)
            cp = remote(
                res.at[pl.ds(peer * lev_dev, lev_dev), pl.ds(t * ROWS, ROWS), :],
                out_ref.at[:, pl.ds(sub * aband + t * ROWS, ROWS), :],
                send2.at[t, off],
                recv2.at[t, off],
                (lon, peer),
            )
            cp.start()
            sends2.append(cp)
        own = pltpu.make_async_copy(
            res.at[pl.ds(sub * lev_dev, lev_dev), pl.ds(t * ROWS, ROWS), :],
            out_ref.at[:, pl.ds(sub * aband + t * ROWS, ROWS), :],
            own_sem.at[1, t],
        )
        own.start()
        sends2.append(own)

    fluxbuf[...] = heat_ref[band, :] * (sst[...] - res[levels - 1])
    flux_ref[...] = fluxbuf[...]
    fcopy = remote(fluxbuf, flux_in, hsend.at[8], hrecv.at[8], (west, sub))
    fcopy.start()
    for cp in ocean_copies[1:]:
        cp.wait()
    fcopy.wait()

    blocks = jnp.concatenate(
        [fluxbuf[:, g * LANES : (g + 1) * LANES] for g in range(groups)]
        + [flux_in[:, g * LANES : (g + 1) * LANES] for g in range(groups)],
        axis=0,
    )
    for k in range(width):
        src = a2o_src_ref[:, 0, :][:, k : k + 1]
        grp = jnp.remainder(src % ngroups - lon * groups, ngroups)
        ids = grp * aband + (src // ngroups - sub * aband)
        apicked[k] = dot(one_hot(ids, 2 * groups * aband), blocks)
    wa = a2o_wgt_ref[:, 0, :]

    def a2o_step(w, acc):
        part = jnp.where(wa[:, 0:1] == w, apicked[0], 0.0)
        for k in range(1, width):
            part = part + jnp.where(wa[:, k : k + 1] == w, apicked[k], 0.0)
        return acc + dot_nt(part, wbuf[w])

    flux_ocean = lax.fori_loop(
        0, nw, a2o_step, jnp.zeros((orows, LANES), jnp.float32), unroll=4
    )

    rev_r = lax.broadcasted_iota(jnp.int32, (LANES, LANES), 0)
    rev_c = lax.broadcasted_iota(jnp.int32, (LANES, LANES), 1)
    rev = jnp.where(rev_r + rev_c == LANES - 1, 1.0, 0.0).astype(jnp.float32)
    folded = dot(edge_in[2], rev)
    s_row = jnp.where(sub == 0, edge[0], edge_in[0])
    n_row = jnp.where(sub == n_sub - 1, folded, edge_in[1])
    edge[0] = s_row
    edge[1] = n_row
    olane = lax.broadcasted_iota(jnp.int32, (orows, LANES), 1)
    orow = lax.broadcasted_iota(jnp.int32, (orows, LANES), 0)
    diff = diff_ref[...]

    def step(l, carry):
        x = ocean_ref[l]
        ow = jnp.where(olane == 0, pltpu.roll(tile_in[0, l], 1, 1), pltpu.roll(x, 1, 1))
        oe = jnp.where(
            olane == LANES - 1,
            pltpu.roll(tile_in[1, l], LANES - 1, 1),
            pltpu.roll(x, LANES - 1, 1),
        )
        so = jnp.where(orow == 0, edge[0, pl.ds(l, 1), :], pltpu.roll(x, 1, 0))
        no = jnp.where(orow == orows - 1, edge[1, pl.ds(l, 1), :], pltpu.roll(x, orows - 1, 0))
        lap = ow + oe + no + so - 4.0 * x
        otmp[l] = maskf * (x + diff * lap)
        return carry

    lax.fori_loop(0, olev, step, 0, unroll=2)
    otmp[0] = otmp[0] + maskf * flux_ocean
    stepped = jnp.swapaxes(otmp[...], 0, 1)
    for r in range(orows):
        otmp2[r] = dot(oinv_ref[...], stepped[r])
    onew_ref[...] = jnp.swapaxes(otmp2[...], 0, 1)

    for cp in sends2:
        cp.wait()


def per_device(
    atm_tracer,
    courant,
    column_inverse,
    heat_exchange_factor,
    ocean_temp,
    diffusivity,
    ocean_inverse,
    land_mask,
    regrid_weight_blocks,
    a2o_src,
    a2o_wgt,
    o2a_src,
    o2a_wgt,
):
    n_lon = lax.axis_size("lon")
    n_sub = lax.axis_size("sub")
    lev_dev, alat, alon = atm_tracer.shape
    levels = lev_dev * n_sub
    aband = alat // n_sub
    nchunk = aband // ROWS
    local_bands = column_inverse.shape[0] // n_sub
    olev, orows, olon = ocean_temp.shape
    groups = alon // LANES
    width = a2o_src.shape[2]
    f32 = jnp.float32
    vm = pl.BlockSpec(memory_space=pltpu.VMEM)
    hbm = pl.BlockSpec(memory_space=pl.ANY)
    return pl.pallas_call(
        functools.partial(kernel, n_lon, n_sub),
        out_shape=(
            jax.ShapeDtypeStruct(atm_tracer.shape, f32),
            jax.ShapeDtypeStruct(ocean_temp.shape, f32),
            jax.ShapeDtypeStruct((aband, alon), f32),
        ),
        in_specs=[hbm, hbm, hbm, vm, vm, vm, vm, vm, hbm, vm, vm, vm, vm],
        out_specs=(hbm, vm, vm),
        scratch_shapes=[
            pltpu.VMEM(atm_tracer.shape, f32),
            pltpu.VMEM(atm_tracer.shape, f32),
            pltpu.VMEM(atm_tracer.shape, f32),
            pltpu.VMEM((levels, aband, alon), f32),
            pltpu.VMEM((levels, aband, alon), f32),
            pltpu.VMEM((ROWS, levels, alon), f32),
            pltpu.VMEM((ROWS, levels, alon), f32),
            pltpu.VMEM(regrid_weight_blocks.shape, f32),
            pltpu.VMEM((local_bands, levels, levels), f32),
            pltpu.VMEM((2, alat, LANES), f32),
            pltpu.VMEM((2, alat, LANES), f32),
            pltpu.VMEM((2, orows, olon), f32),
            pltpu.VMEM((2, olev, orows, olon), f32),
            pltpu.VMEM((2, olev, olon), f32),
            pltpu.VMEM((3, olev, olon), f32),
            pltpu.VMEM((aband, alon), f32),
            pltpu.VMEM((aband, alon), f32),
            pltpu.VMEM((width, groups * aband, LANES), f32),
            pltpu.VMEM((width, orows, LANES), f32),
            pltpu.VMEM((aband, alon), f32),
            pltpu.VMEM((olev, orows, olon), f32),
            pltpu.VMEM((orows, olev, olon), f32),
            pltpu.SemaphoreType.DMA((4,)),
            pltpu.SemaphoreType.DMA((2, nchunk)),
            pltpu.SemaphoreType.DMA((nchunk, n_sub)),
            pltpu.SemaphoreType.DMA((nchunk, n_sub)),
            pltpu.SemaphoreType.DMA((nchunk, n_sub)),
            pltpu.SemaphoreType.DMA((nchunk, n_sub)),
            pltpu.SemaphoreType.DMA((9,)),
            pltpu.SemaphoreType.DMA((9,)),
        ],
        compiler_params=pltpu.CompilerParams(
            collective_id=0, has_side_effects=True, vmem_limit_bytes=48 * 1024 * 1024
        ),
        name="step",
    )(
        atm_tracer,
        courant,
        column_inverse,
        heat_exchange_factor,
        ocean_temp,
        diffusivity,
        ocean_inverse,
        land_mask,
        regrid_weight_blocks,
        a2o_src,
        a2o_wgt,
        o2a_src,
        o2a_wgt,
    )


def solution(mesh):
    return jax.shard_map(
        per_device,
        mesh=mesh,
        in_specs=(
            P("sub", None, "lon"),
            P("sub", None, "lon"),
            P(),
            P(None, "lon"),
            P(None, "sub", "lon"),
            P("sub", "lon"),
            P(),
            P("sub", "lon"),
            P(),
            P("sub", "lon", None),
            P("sub", "lon", None),
            P(None, "lon", None),
            P(None, "lon", None),
        ),
        out_specs=(P("sub", None, "lon"), P(None, "sub", "lon"), P("sub", "lon")),
        check_vma=False,
    )
```

```python
import functools

import jax
import jax.numpy as jnp
from jax import lax
from jax.experimental import pallas as pl
from jax.experimental.pallas import tpu as pltpu
from jax.sharding import PartitionSpec as P

HI = lax.Precision.HIGHEST
MESH = pl.DeviceIdType.MESH
ROWS = 8
LANES = 128
WRITES = 4


def dot(a, b):
    return jnp.dot(a, b, precision=HI, preferred_element_type=jnp.float32)


def dot_nt(a, b):
    return lax.dot_general(
        a, b, (((1,), (1,)), ((), ())), precision=HI, preferred_element_type=jnp.float32
    )


def one_hot(ids, count):
    cols = lax.broadcasted_iota(jnp.int32, (ids.shape[0], count), 1)
    return jnp.where(cols == ids, 1.0, 0.0).astype(jnp.float32)


def kernel(
    n_lon,
    n_sub,
    atm_hbm,
    cour_hbm,
    colinv_hbm,
    heat_hbm,
    ocean_hbm,
    diff_hbm,
    oinv_hbm,
    mask_hbm,
    w_hbm,
    a2o_src_hbm,
    a2o_wgt_hbm,
    o2a_src_hbm,
    o2a_wgt_hbm,
    out_ref,
    onew_ref,
    flux_ref,
    xbuf,
    cbuf,
    adv,
    cols,
    res,
    tmp,
    tmp2,
    wbuf,
    inv,
    heat_ref,
    ocean_ref,
    diff_ref,
    oinv_ref,
    mask_ref,
    a2o_src_ref,
    a2o_wgt_ref,
    o2a_src_ref,
    o2a_wgt_ref,
    ids_a,
    ids_o,
    halo,
    halo_in,
    sea,
    tile_in,
    edge,
    edge_in,
    fluxbuf,
    flux_in,
    picked,
    apicked,
    sst,
    otmp,
    otmp2,
    local_sem,
    load_sem,
    own_sem,
    xsend,
    xrecv,
    send1,
    recv1,
    send2,
    recv2,
    hsend,
    hrecv,
):
    lon = lax.axis_index("lon")
    sub = lax.axis_index("sub")
    lev_dev, _, aband, alon = xbuf.shape
    levels = lev_dev * n_sub
    nchunk = aband // ROWS
    local_bands = inv.shape[0]
    rows_band = aband // local_bands
    groups = alon // LANES
    ngroups = groups * n_lon
    olev, orows, _ = ocean_ref.shape
    nw = wbuf.shape[0]
    width = a2o_src_ref.shape[1]

    east = lax.rem(lon + 1, n_lon)
    west = lax.rem(lon + n_lon - 1, n_lon)
    mirror = n_lon - 1 - lon
    north = lax.rem(sub + 1, n_sub)
    south = lax.rem(sub + n_sub - 1, n_sub)

    load_x = []
    load_c = []
    for t in range(nchunk):
        part = pl.ds(t * ROWS, ROWS)
        for hbm, buf, loads, i in ((atm_hbm, xbuf, load_x, 0), (cour_hbm, cbuf, load_c, 1)):
            cp = pltpu.make_async_copy(
                hbm.at[:, :, part, :], buf.at[:, :, part, :], load_sem.at[i, t]
            )
            cp.start()
            loads.append(cp)
    small = [
        pltpu.make_async_copy(hbm, buf, local_sem.at[i])
        for i, (hbm, buf) in enumerate(
            (
                (ocean_hbm, ocean_ref),
                (mask_hbm, mask_ref),
                (colinv_hbm.at[pl.ds(sub * local_bands, local_bands)], inv),
                (heat_hbm.at[pl.ds(sub * aband, aband)], heat_ref),
                (diff_hbm, diff_ref),
                (oinv_hbm, oinv_ref),
                (a2o_src_hbm, a2o_src_ref),
                (a2o_wgt_hbm, a2o_wgt_ref),
                (o2a_src_hbm, o2a_src_ref),
                (o2a_wgt_hbm, o2a_wgt_ref),
                (w_hbm, wbuf),
            )
        )
    ]
    for cp in small:
        cp.start()

    barrier = pltpu.get_barrier_semaphore()
    for target in (east, west, mirror):
        pl.semaphore_signal(barrier, inc=1, device_id=(target, sub), device_id_type=MESH)
    for off in range(1, n_sub):
        peer = lax.rem(sub + off, n_sub)
        pl.semaphore_signal(barrier, inc=1, device_id=(lon, peer), device_id_type=MESH)

    def remote(src, dst, ssem, rsem, target):
        return pltpu.make_async_remote_copy(
            src_ref=src, dst_ref=dst, send_sem=ssem, recv_sem=rsem,
            device_id=target, device_id_type=MESH,
        )

    lane = lax.broadcasted_iota(jnp.int32, (n_sub, ROWS, LANES), 2)

    def pack(t):
        rows = slice(t * ROWS, (t + 1) * ROWS)

        def body(l, carry):
            tail, head = carry
            last = xbuf[l, :, rows, alon - LANES :]
            first = xbuf[l, :, rows, :LANES]
            tail = jnp.where(lane == l, pltpu.roll(last, lax.rem(l + 1, LANES), 2), tail)
            head = jnp.where(lane == l, pltpu.roll(first, l, 2), head)
            return tail, head

        load_x[t].wait()
        zero = jnp.zeros((n_sub, ROWS, LANES), jnp.float32)
        tail, head = lax.fori_loop(0, lev_dev, body, (zero, zero), unroll=8)
        halo[0, t] = tail
        halo[1, t] = head

    def halo_copies(t):
        pair = [
            remote(halo.at[i, t], halo_in.at[i, t], xsend.at[i, t], xrecv.at[i, t], (side, sub))
            for i, side in ((0, east), (1, west))
        ]
        for cp in pair:
            cp.start()
        return pair

    pack(0)
    pl.semaphore_wait(barrier, 3 + n_sub - 1)
    halos = [halo_copies(0)]
    for t in range(1, nchunk):
        pack(t)
        halos.append(halo_copies(t))

    wide = lax.broadcasted_iota(jnp.int32, (ROWS, alon), 1)

    def advect(d, t, write):
        rows = slice(t * ROWS, (t + 1) * ROWS)
        from_west = halo_in[0, t, d]
        from_east = halo_in[1, t, d]

        def body(l, carry):
            x = xbuf[l, d, rows, :]
            c = cbuf[l, d, rows, :]
            hw = pltpu.roll(from_west, lax.rem(LANES - l, LANES), 1)
            he = pltpu.roll(from_east, LANES - 1 - l, 1)
            edges = jnp.concatenate([hw] * (groups - 1) + [he], axis=1)
            xw = jnp.where(wide == 0, edges, pltpu.roll(x, 1, 1))
            xe = jnp.where(wide == alon - 1, edges, pltpu.roll(x, alon - 1, 1))
            write(l, x - jnp.maximum(c, 0.0) * (x - xw) - jnp.minimum(c, 0.0) * (xe - x))
            return carry

        lax.fori_loop(0, lev_dev, body, 0, unroll=8)

    offs = [n_sub // 2] + [o for o in range(n_sub - 1, 0, -1) if o != n_sub // 2]
    sends1 = []
    for t in range(nchunk):
        load_c[t].wait()
        for cp in halos[t]:
            cp.wait()
        rows = slice(t * ROWS, (t + 1) * ROWS)
        for off in offs:
            peer = lax.rem(sub + off, n_sub)

            def keep(l, value, peer=peer, rows=rows):
                adv[l, peer, rows, :] = value

            advect(peer, t, keep)
            cp = remote(
                adv.at[:, peer, pl.ds(t * ROWS, ROWS), :],
                cols.at[pl.ds(sub * lev_dev, lev_dev), pl.ds(t * ROWS, ROWS), :],
                send1.at[t, off],
                recv1.at[t, off],
                (lon, peer),
            )
            cp.start()
            sends1.append((t, cp))

        def keep_own(l, value, rows=rows):
            cols[sub * lev_dev + l, rows, :] = value

        advect(sub, t, keep_own)

    for cp in small[:2]:
        cp.wait()
    maskf = mask_ref[...].astype(jnp.float32)
    sea[0] = maskf * ocean_ref[0]
    edge[0] = ocean_ref[:, 0, :]
    edge[1] = ocean_ref[:, orows - 1, :]
    ocean_copies = [
        remote(sea.at[0], sea.at[1], hsend.at[2], hrecv.at[2], (east, sub)),
        remote(ocean_ref, tile_in.at[0], hsend.at[3], hrecv.at[3], (east, sub)),
        remote(ocean_ref, tile_in.at[1], hsend.at[4], hrecv.at[4], (west, sub)),
        remote(edge.at[1], edge_in.at[0], hsend.at[5], hrecv.at[5], (lon, north)),
        remote(edge.at[0], edge_in.at[1], hsend.at[6], hrecv.at[6], (lon, south)),
        remote(edge.at[1], edge_in.at[2], hsend.at[7], hrecv.at[7], (mirror, sub)),
    ]
    for cp in ocean_copies:
        cp.start()
    for cp in small[2:]:
        cp.wait()
    for g in range(groups):
        pair = jnp.concatenate([o2a_src_ref[g], o2a_wgt_ref[g]], axis=0)
        ids_a[g] = jnp.transpose(pair, (1, 0))
    ids_o[...] = jnp.zeros_like(ids_o)
    ids_o[:width, :orows] = a2o_src_ref[0]
    ids_o[width : 2 * width, :orows] = a2o_wgt_ref[0]
    ids_ocean = jnp.transpose(ids_o[...], (1, 0))[:orows]

    ocean_copies[0].wait()
    window = jnp.concatenate([sea[1], sea[0]], axis=0)
    band = pl.ds(sub * aband, aband)
    for g in range(groups):
        for k in range(width):
            src = ids_a[g, band, :][:, k : k + 1]
            tile = jnp.remainder(src % n_lon - lon + 1, n_lon)
            ids = tile * orows + (src // n_lon - sub * orows)
            picked[k, g * aband : (g + 1) * aband, :] = dot(one_hot(ids, 2 * orows), window)
    wg = jnp.concatenate([ids_a[g, band, :][:, width:] for g in range(groups)], axis=0)

    def sst_step(w, acc):
        part = jnp.where(wg[:, 0:1] == w, picked[0], 0.0)
        for k in range(1, width):
            part = part + jnp.where(wg[:, k : k + 1] == w, picked[k], 0.0)
        return acc + dot_nt(part, wbuf[w])

    acc = lax.fori_loop(
        0, nw, sst_step, jnp.zeros((groups * aband, LANES), jnp.float32), unroll=2
    )
    for g in range(groups):
        sst[:, g * LANES : (g + 1) * LANES] = acc[g * aband : (g + 1) * aband]

    sends2 = []
    for t in range(nchunk):
        for tt, cp in sends1:
            if tt == t:
                cp.wait()
        rows = slice(t * ROWS, (t + 1) * ROWS)

        def turn(i, carry, rows=rows):
            part = cols[pl.ds(i * ROWS, ROWS), rows, :]
            tmp[:, pl.ds(i * ROWS, ROWS), :] = jnp.swapaxes(part, 0, 1)
            return carry

        lax.fori_loop(0, levels // ROWS, turn, 0, unroll=2)

        def solve(r, carry, t=t):
            tmp2[r] = dot(inv[t * ROWS // rows_band], tmp[r])
            return carry

        lax.fori_loop(0, ROWS, solve, 0)

        def back(i, carry, rows=rows):
            part = tmp2[:, pl.ds(i * ROWS, ROWS), :]
            res[pl.ds(i * ROWS, ROWS), rows, :] = jnp.swapaxes(part, 0, 1)
            return carry

        lax.fori_loop(0, levels // ROWS, back, 0, unroll=2)
        for off in offs:
            peer = lax.rem(sub + off, n_sub)
            cp = remote(
                res.at[pl.ds(peer * lev_dev, lev_dev), pl.ds(t * ROWS, ROWS), :],
                out_ref.at[:, pl.ds(sub * aband + t * ROWS, ROWS), :],
                send2.at[t, off],
                recv2.at[t, off],
                (lon, peer),
            )
            cp.start()
            sends2.append(cp)
        own = pltpu.make_async_copy(
            res.at[pl.ds(sub * lev_dev, lev_dev), pl.ds(t * ROWS, ROWS), :],
            out_ref.at[:, pl.ds(sub * aband + t * ROWS, ROWS), :],
            own_sem.at[t],
        )
        own.start()
        sends2.append(own)

    fluxbuf[...] = heat_ref[...] * (sst[...] - res[levels - 1])
    flux_ref[...] = fluxbuf[...]
    fcopy = remote(fluxbuf, flux_in, hsend.at[8], hrecv.at[8], (west, sub))
    fcopy.start()
    for cp in ocean_copies[1:]:
        cp.wait()
    fcopy.wait()

    blocks = jnp.concatenate(
        [fluxbuf[:, g * LANES : (g + 1) * LANES] for g in range(groups)]
        + [flux_in[:, g * LANES : (g + 1) * LANES] for g in range(groups)],
        axis=0,
    )
    for k in range(width):
        src = ids_ocean[:, k : k + 1]
        grp = jnp.remainder(src % ngroups - lon * groups, ngroups)
        ids = grp * aband + (src // ngroups - sub * aband)
        apicked[k] = dot(one_hot(ids, 2 * groups * aband), blocks)
    wa = ids_ocean[:, width:]

    def a2o_step(w, acc):
        part = jnp.where(wa[:, 0:1] == w, apicked[0], 0.0)
        for k in range(1, width):
            part = part + jnp.where(wa[:, k : k + 1] == w, apicked[k], 0.0)
        return acc + dot_nt(part, wbuf[w])

    flux_ocean = lax.fori_loop(
        0, nw, a2o_step, jnp.zeros((orows, LANES), jnp.float32), unroll=4
    )

    rev_r = lax.broadcasted_iota(jnp.int32, (LANES, LANES), 0)
    rev_c = lax.broadcasted_iota(jnp.int32, (LANES, LANES), 1)
    rev = jnp.where(rev_r + rev_c == LANES - 1, 1.0, 0.0).astype(jnp.float32)
    folded = dot(edge_in[2], rev)
    s_row = jnp.where(sub == 0, edge[0], edge_in[0])
    n_row = jnp.where(sub == n_sub - 1, folded, edge_in[1])
    edge[0] = s_row
    edge[1] = n_row
    olane = lax.broadcasted_iota(jnp.int32, (orows, LANES), 1)
    orow = lax.broadcasted_iota(jnp.int32, (orows, LANES), 0)
    diff = diff_ref[...]

    def step(l, carry):
        x = ocean_ref[l]
        ow = jnp.where(olane == 0, pltpu.roll(tile_in[0, l], 1, 1), pltpu.roll(x, 1, 1))
        oe = jnp.where(
            olane == LANES - 1,
            pltpu.roll(tile_in[1, l], LANES - 1, 1),
            pltpu.roll(x, LANES - 1, 1),
        )
        so = jnp.where(orow == 0, edge[0, pl.ds(l, 1), :], pltpu.roll(x, 1, 0))
        no = jnp.where(orow == orows - 1, edge[1, pl.ds(l, 1), :], pltpu.roll(x, orows - 1, 0))
        lap = ow + oe + no + so - 4.0 * x
        otmp[l] = maskf * (x + diff * lap)
        return carry

    lax.fori_loop(0, olev, step, 0, unroll=2)
    otmp[0] = otmp[0] + maskf * flux_ocean
    stepped = jnp.swapaxes(otmp[...], 0, 1)
    for r in range(orows):
        otmp2[r] = dot(oinv_ref[...], stepped[r])
    onew_ref[...] = jnp.swapaxes(otmp2[...], 0, 1)

    for cp in sends2:
        cp.wait()


def write_out(air, ocean, flux, air_out, ocean_out, flux_out, sem):
    step = air.shape[0] // WRITES
    copies = [
        pltpu.make_async_copy(
            air.at[pl.ds(i * step, step)], air_out.at[pl.ds(i * step, step)], sem.at[i]
        )
        for i in range(WRITES)
    ]
    copies.append(pltpu.make_async_copy(ocean, ocean_out, sem.at[WRITES]))
    copies.append(pltpu.make_async_copy(flux, flux_out, sem.at[WRITES + 1]))
    for cp in copies:
        cp.start()
    for cp in copies:
        cp.wait()


def per_device(
    atm_tracer,
    courant,
    column_inverse,
    heat_exchange_factor,
    ocean_temp,
    diffusivity,
    ocean_inverse,
    land_mask,
    regrid_weight_blocks,
    a2o_src,
    a2o_wgt,
    o2a_src,
    o2a_wgt,
):
    n_lon = lax.axis_size("lon")
    n_sub = lax.axis_size("sub")
    lev_dev, alat, alon = atm_tracer.shape
    levels = lev_dev * n_sub
    aband = alat // n_sub
    nchunk = aband // ROWS
    local_bands = column_inverse.shape[0] // n_sub
    olev, orows, olon = ocean_temp.shape
    groups = alon // LANES
    width = a2o_src.shape[2]
    f32 = jnp.float32
    vm = pl.BlockSpec(memory_space=pltpu.VMEM)
    hbm = pl.BlockSpec(memory_space=pltpu.HBM)
    anywhere = pl.BlockSpec(memory_space=pl.ANY)
    results = pl.pallas_call(
        functools.partial(kernel, n_lon, n_sub),
        out_shape=(
            pltpu.VMEM(atm_tracer.shape, f32),
            pltpu.VMEM(ocean_temp.shape, f32),
            pltpu.VMEM((aband, alon), f32),
        ),
        in_specs=[hbm] * 13,
        out_specs=(anywhere, vm, vm),
        scratch_shapes=[
            pltpu.VMEM((lev_dev, n_sub, aband, alon), f32),
            pltpu.VMEM((lev_dev, n_sub, aband, alon), f32),
            pltpu.VMEM((lev_dev, n_sub, aband, alon), f32),
            pltpu.VMEM((levels, aband, alon), f32),
            pltpu.VMEM((levels, aband, alon), f32),
            pltpu.VMEM((ROWS, levels, alon), f32),
            pltpu.VMEM((ROWS, levels, alon), f32),
            pltpu.VMEM(regrid_weight_blocks.shape, f32),
            pltpu.VMEM((local_bands, levels, levels), f32),
            pltpu.VMEM((aband, alon), f32),
            pltpu.VMEM(ocean_temp.shape, f32),
            pltpu.VMEM(diffusivity.shape, f32),
            pltpu.VMEM(ocean_inverse.shape, f32),
            pltpu.VMEM(land_mask.shape, jnp.int32),
            pltpu.VMEM((1, width, orows), jnp.int32),
            pltpu.VMEM((1, width, orows), jnp.int32),
            pltpu.VMEM((groups, width, alat), jnp.int32),
            pltpu.VMEM((groups, width, alat), jnp.int32),
            pltpu.VMEM((groups, alat, 2 * width), jnp.int32),
            pltpu.VMEM((2 * width, LANES), jnp.int32),
            pltpu.VMEM((2, nchunk, n_sub, ROWS, LANES), f32),
            pltpu.VMEM((2, nchunk, n_sub, ROWS, LANES), f32),
            pltpu.VMEM((2, orows, olon), f32),
            pltpu.VMEM((2, olev, orows, olon), f32),
            pltpu.VMEM((2, olev, olon), f32),
            pltpu.VMEM((3, olev, olon), f32),
            pltpu.VMEM((aband, alon), f32),
            pltpu.VMEM((aband, alon), f32),
            pltpu.VMEM((width, groups * aband, LANES), f32),
            pltpu.VMEM((width, orows, LANES), f32),
            pltpu.VMEM((aband, alon), f32),
            pltpu.VMEM((olev, orows, olon), f32),
            pltpu.VMEM((orows, olev, olon), f32),
            pltpu.SemaphoreType.DMA((11,)),
            pltpu.SemaphoreType.DMA((2, nchunk)),
            pltpu.SemaphoreType.DMA((nchunk,)),
            pltpu.SemaphoreType.DMA((2, nchunk)),
            pltpu.SemaphoreType.DMA((2, nchunk)),
            pltpu.SemaphoreType.DMA((nchunk, n_sub)),
            pltpu.SemaphoreType.DMA((nchunk, n_sub)),
            pltpu.SemaphoreType.DMA((nchunk, n_sub)),
            pltpu.SemaphoreType.DMA((nchunk, n_sub)),
            pltpu.SemaphoreType.DMA((9,)),
            pltpu.SemaphoreType.DMA((9,)),
        ],
        compiler_params=pltpu.CompilerParams(
            collective_id=0, has_side_effects=True, vmem_limit_bytes=48 * 1024 * 1024
        ),
        name="step",
    )(*(pltpu.with_memory_space_constraint(v, pltpu.HBM) for v in (
        atm_tracer.reshape(lev_dev, n_sub, aband, alon),
        courant.reshape(lev_dev, n_sub, aband, alon),
        column_inverse,
        heat_exchange_factor,
        ocean_temp,
        diffusivity,
        ocean_inverse,
        land_mask,
        regrid_weight_blocks,
        jnp.transpose(a2o_src, (1, 2, 0)),
        jnp.transpose(a2o_wgt, (1, 2, 0)),
        jnp.transpose(o2a_src, (1, 2, 0)),
        jnp.transpose(o2a_wgt, (1, 2, 0)),
    )))
    return pl.pallas_call(
        write_out,
        out_shape=[jax.ShapeDtypeStruct(v.shape, f32) for v in results],
        in_specs=[anywhere] * 3,
        out_specs=[hbm] * 3,
        scratch_shapes=[pltpu.SemaphoreType.DMA((WRITES + 2,))],
        compiler_params=pltpu.CompilerParams(vmem_limit_bytes=1024 * 1024),
        name="write_out",
    )(*results)


def solution(mesh):
    return jax.shard_map(
        per_device,
        mesh=mesh,
        in_specs=(
            P("sub", None, "lon"),
            P("sub", None, "lon"),
            P(),
            P(None, "lon"),
            P(None, "sub", "lon"),
            P("sub", "lon"),
            P(),
            P("sub", "lon"),
            P(),
            P("sub", "lon", None),
            P("sub", "lon", None),
            P(None, "lon", None),
            P(None, "lon", None),
        ),
        out_specs=(P("sub", None, "lon"), P(None, "sub", "lon"), P("sub", "lon")),
        check_vma=False,
    )
```

```python
import functools

import jax
import jax.numpy as jnp
from jax import lax
from jax.experimental import pallas as pl
from jax.experimental.pallas import tpu as pltpu
from jax.sharding import PartitionSpec as P

HI = lax.Precision.HIGHEST
MESH = pl.DeviceIdType.MESH
ROWS = 8
LANES = 128
WRITES = 16


def dot(a, b):
    return jnp.dot(a, b, precision=HI, preferred_element_type=jnp.float32)


def dot_nt(a, b):
    return lax.dot_general(
        a, b, (((1,), (1,)), ((), ())), precision=HI, preferred_element_type=jnp.float32
    )


def one_hot(ids, count):
    cols = lax.broadcasted_iota(jnp.int32, (ids.shape[0], count), 1)
    return jnp.where(cols == ids, 1.0, 0.0).astype(jnp.float32)


def kernel(
    n_lon,
    n_sub,
    atm_hbm,
    cour_hbm,
    colinv_hbm,
    heat_hbm,
    ocean_hbm,
    diff_hbm,
    oinv_hbm,
    mask_hbm,
    w_hbm,
    a2o_src_hbm,
    a2o_wgt_hbm,
    o2a_src_hbm,
    o2a_wgt_hbm,
    out_ref,
    onew_ref,
    flux_ref,
    xbuf,
    cbuf,
    adv,
    cols,
    res,
    tmp,
    tmp2,
    wbuf,
    inv,
    heat_ref,
    ocean_ref,
    diff_ref,
    oinv_ref,
    mask_ref,
    a2o_src_ref,
    a2o_wgt_ref,
    o2a_src_ref,
    o2a_wgt_ref,
    ids_a,
    ids_o,
    halo,
    halo_in,
    corr,
    corr_in,
    sea,
    tile_in,
    edge,
    edge_in,
    fluxbuf,
    flux_in,
    picked,
    apicked,
    sst,
    otmp,
    otmp2,
    local_sem,
    load_sem,
    own_sem,
    xsend,
    xrecv,
    csend,
    crecv,
    send1,
    recv1,
    send2,
    recv2,
    hsend,
    hrecv,
):
    lon = lax.axis_index("lon")
    sub = lax.axis_index("sub")
    lev_dev, _, aband, alon = xbuf.shape
    levels = lev_dev * n_sub
    nchunk = aband // ROWS
    local_bands = inv.shape[0]
    rows_band = aband // local_bands
    groups = alon // LANES
    ngroups = groups * n_lon
    olev, orows, _ = ocean_ref.shape
    nw = wbuf.shape[0]
    width = a2o_src_ref.shape[1]

    east = lax.rem(lon + 1, n_lon)
    west = lax.rem(lon + n_lon - 1, n_lon)
    mirror = n_lon - 1 - lon
    north = lax.rem(sub + 1, n_sub)
    south = lax.rem(sub + n_sub - 1, n_sub)

    load_x = []
    load_c = []
    for t in range(nchunk):
        part = pl.ds(t * ROWS, ROWS)
        for hbm, buf, loads, i in ((atm_hbm, xbuf, load_x, 0), (cour_hbm, cbuf, load_c, 1)):
            cp = pltpu.make_async_copy(
                hbm.at[:, :, part, :], buf.at[:, :, part, :], load_sem.at[i, t]
            )
            cp.start()
            loads.append(cp)
    small = [
        pltpu.make_async_copy(hbm, buf, local_sem.at[i])
        for i, (hbm, buf) in enumerate(
            (
                (ocean_hbm, ocean_ref),
                (mask_hbm, mask_ref),
                (colinv_hbm.at[pl.ds(sub * local_bands, local_bands)], inv),
                (heat_hbm.at[pl.ds(sub * aband, aband)], heat_ref),
                (diff_hbm, diff_ref),
                (oinv_hbm, oinv_ref),
                (a2o_src_hbm, a2o_src_ref),
                (a2o_wgt_hbm, a2o_wgt_ref),
                (o2a_src_hbm, o2a_src_ref),
                (o2a_wgt_hbm, o2a_wgt_ref),
                (w_hbm, wbuf),
            )
        )
    ]
    for cp in small:
        cp.start()

    barrier = pltpu.get_barrier_semaphore()
    for target in (east, west, mirror):
        pl.semaphore_signal(barrier, inc=1, device_id=(target, sub), device_id_type=MESH)
    for off in range(1, n_sub):
        peer = lax.rem(sub + off, n_sub)
        pl.semaphore_signal(barrier, inc=1, device_id=(lon, peer), device_id_type=MESH)

    def remote(src, dst, ssem, rsem, target):
        return pltpu.make_async_remote_copy(
            src_ref=src, dst_ref=dst, send_sem=ssem, recv_sem=rsem,
            device_id=target, device_id_type=MESH,
        )

    lane = lax.broadcasted_iota(jnp.int32, (n_sub, ROWS, LANES), 2)

    def pack(buf, t):
        rows = slice(t * ROWS, (t + 1) * ROWS)

        def body(l, carry):
            tail, head = carry
            last = buf[l, :, rows, alon - LANES :]
            first = buf[l, :, rows, :LANES]
            tail = jnp.where(lane == l, pltpu.roll(last, lax.rem(l + 1, LANES), 2), tail)
            head = jnp.where(lane == l, pltpu.roll(first, l, 2), head)
            return tail, head

        zero = jnp.zeros((n_sub, ROWS, LANES), jnp.float32)
        return lax.fori_loop(0, lev_dev, body, (zero, zero), unroll=8)

    def halo_copies(t):
        tail, head = pack(xbuf, t)
        halo[0, t] = tail
        halo[1, t] = head
        pair = [
            remote(halo.at[i, t], halo_in.at[i, t], xsend.at[i, t], xrecv.at[i, t], (side, sub))
            for i, side in ((0, east), (1, west))
        ]
        for cp in pair:
            cp.start()
        return pair

    wide = lax.broadcasted_iota(jnp.int32, (ROWS, alon), 1)

    def advect(d, t, write):
        rows = slice(t * ROWS, (t + 1) * ROWS)

        def body(l, carry):
            x = xbuf[l, d, rows, :]
            c = cbuf[l, d, rows, :]
            if t == 0:
                edges = 0.0
            else:
                hw = pltpu.roll(halo_in[0, t, d], lax.rem(LANES - l, LANES), 1)
                he = pltpu.roll(halo_in[1, t, d], LANES - 1 - l, 1)
                edges = jnp.concatenate([hw] * (groups - 1) + [he], axis=1)
            xw = jnp.where(wide == 0, edges, pltpu.roll(x, 1, 1))
            xe = jnp.where(wide == alon - 1, edges, pltpu.roll(x, alon - 1, 1))
            write(l, x - jnp.maximum(c, 0.0) * (x - xw) - jnp.minimum(c, 0.0) * (xe - x))
            return carry

        lax.fori_loop(0, lev_dev, body, 0, unroll=8)

    offs = [n_sub // 2] + [o for o in range(n_sub - 1, 0, -1) if o != n_sub // 2]
    sends1 = []

    def advect_to(off, t):
        peer = lax.rem(sub + off, n_sub)
        rows = slice(t * ROWS, (t + 1) * ROWS)

        def keep(l, value):
            adv[l, peer, rows, :] = value

        advect(peer, t, keep)

    def send_to(off, t):
        peer = lax.rem(sub + off, n_sub)
        cp = remote(
            adv.at[:, peer, pl.ds(t * ROWS, ROWS), :],
            cols.at[pl.ds(sub * lev_dev, lev_dev), pl.ds(t * ROWS, ROWS), :],
            send1.at[t, off],
            recv1.at[t, off],
            (lon, peer),
        )
        cp.start()
        sends1.append((t, cp))

    def advect_own(t):
        rows = slice(t * ROWS, (t + 1) * ROWS)

        def keep(l, value):
            cols[sub * lev_dev + l, rows, :] = value

        advect(sub, t, keep)

    load_x[0].wait()
    load_c[0].wait()
    for off in offs:
        advect_to(off, 0)
    pl.semaphore_wait(barrier, 3 + n_sub - 1)
    for off in offs:
        send_to(off, 0)
    halos = [halo_copies(0)]
    for t in range(1, nchunk):
        load_x[t].wait()
        halos.append(halo_copies(t))
    advect_own(0)
    ctail, chead = pack(cbuf, 0)
    for cp in halos[0]:
        cp.wait()
    share_west = jnp.maximum(chead, 0.0) * halo_in[0, 0]
    share_east = -jnp.minimum(ctail, 0.0) * halo_in[1, 0]
    for d in range(n_sub):
        corr[d, 0] = share_west[d]
        corr[d, 1] = share_east[d]
    shares = []
    for off in offs:
        peer = lax.rem(sub + off, n_sub)
        cp = remote(
            corr.at[peer], corr_in.at[sub], csend.at[off], crecv.at[off], (lon, peer)
        )
        cp.start()
        shares.append(cp)
    corr_in[sub] = corr[sub]
    for t in range(1, nchunk):
        load_c[t].wait()
        for cp in halos[t]:
            cp.wait()
        for off in offs:
            advect_to(off, t)
            send_to(off, t)
        advect_own(t)

    for cp in small[:2]:
        cp.wait()
    maskf = mask_ref[...].astype(jnp.float32)
    sea[0] = maskf * ocean_ref[0]
    edge[0] = ocean_ref[:, 0, :]
    edge[1] = ocean_ref[:, orows - 1, :]
    ocean_copies = [
        remote(sea.at[0], sea.at[1], hsend.at[2], hrecv.at[2], (east, sub)),
        remote(ocean_ref, tile_in.at[0], hsend.at[3], hrecv.at[3], (east, sub)),
        remote(ocean_ref, tile_in.at[1], hsend.at[4], hrecv.at[4], (west, sub)),
        remote(edge.at[1], edge_in.at[0], hsend.at[5], hrecv.at[5], (lon, north)),
        remote(edge.at[0], edge_in.at[1], hsend.at[6], hrecv.at[6], (lon, south)),
        remote(edge.at[1], edge_in.at[2], hsend.at[7], hrecv.at[7], (mirror, sub)),
    ]
    for cp in ocean_copies:
        cp.start()
    for cp in small[2:]:
        cp.wait()
    for g in range(groups):
        pair = jnp.concatenate([o2a_src_ref[g], o2a_wgt_ref[g]], axis=0)
        ids_a[g] = jnp.transpose(pair, (1, 0))
    ids_o[...] = jnp.zeros_like(ids_o)
    ids_o[:width, :orows] = a2o_src_ref[0]
    ids_o[width : 2 * width, :orows] = a2o_wgt_ref[0]
    ids_ocean = jnp.transpose(ids_o[...], (1, 0))[:orows]

    ocean_copies[0].wait()
    window = jnp.concatenate([sea[1], sea[0]], axis=0)
    band = pl.ds(sub * aband, aband)
    for g in range(groups):
        for k in range(width):
            src = ids_a[g, band, :][:, k : k + 1]
            tile = jnp.remainder(src % n_lon - lon + 1, n_lon)
            ids = tile * orows + (src // n_lon - sub * orows)
            picked[k, g * aband : (g + 1) * aband, :] = dot(one_hot(ids, 2 * orows), window)
    wg = jnp.concatenate([ids_a[g, band, :][:, width:] for g in range(groups)], axis=0)

    def sst_step(w, acc):
        part = jnp.where(wg[:, 0:1] == w, picked[0], 0.0)
        for k in range(1, width):
            part = part + jnp.where(wg[:, k : k + 1] == w, picked[k], 0.0)
        return acc + dot_nt(part, wbuf[w])

    acc = lax.fori_loop(
        0, nw, sst_step, jnp.zeros((groups * aband, LANES), jnp.float32), unroll=2
    )
    for g in range(groups):
        sst[:, g * LANES : (g + 1) * LANES] = acc[g * aband : (g + 1) * aband]

    sends2 = []
    for t in range(nchunk):
        for tt, cp in sends1:
            if tt == t:
                cp.wait()
        if t == 0:
            for cp in shares:
                cp.wait()
            for s in range(n_sub):

                def add_share(l, carry, s=s):
                    w = pltpu.roll(corr_in[s, 0], lax.rem(LANES - l, LANES), 1)
                    e = pltpu.roll(corr_in[s, 1], LANES - 1 - l, 1)
                    both = jnp.concatenate([w] * (groups - 1) + [e], axis=1)
                    ends = (wide == 0) | (wide == alon - 1)
                    old = cols[s * lev_dev + l, :ROWS, :]
                    cols[s * lev_dev + l, :ROWS, :] = old + jnp.where(ends, both, 0.0)
                    return carry

                lax.fori_loop(0, lev_dev, add_share, 0, unroll=4)
        rows = slice(t * ROWS, (t + 1) * ROWS)

        def turn(i, carry, rows=rows):
            part = cols[pl.ds(i * ROWS, ROWS), rows, :]
            tmp[:, pl.ds(i * ROWS, ROWS), :] = jnp.swapaxes(part, 0, 1)
            return carry

        lax.fori_loop(0, levels // ROWS, turn, 0, unroll=2)

        def solve(r, carry, t=t):
            tmp2[r] = dot(inv[t * ROWS // rows_band], tmp[r])
            return carry

        lax.fori_loop(0, ROWS, solve, 0)

        def back(i, carry, rows=rows):
            part = tmp2[:, pl.ds(i * ROWS, ROWS), :]
            res[pl.ds(i * ROWS, ROWS), rows, :] = jnp.swapaxes(part, 0, 1)
            return carry

        lax.fori_loop(0, levels // ROWS, back, 0, unroll=2)
        for off in offs:
            peer = lax.rem(sub + off, n_sub)
            cp = remote(
                res.at[pl.ds(peer * lev_dev, lev_dev), pl.ds(t * ROWS, ROWS), :],
                out_ref.at[:, pl.ds(sub * aband + t * ROWS, ROWS), :],
                send2.at[t, off],
                recv2.at[t, off],
                (lon, peer),
            )
            cp.start()
            sends2.append(cp)
        own = pltpu.make_async_copy(
            res.at[pl.ds(sub * lev_dev, lev_dev), pl.ds(t * ROWS, ROWS), :],
            out_ref.at[:, pl.ds(sub * aband + t * ROWS, ROWS), :],
            own_sem.at[t],
        )
        own.start()
        sends2.append(own)

    fluxbuf[...] = heat_ref[...] * (sst[...] - res[levels - 1])
    flux_ref[...] = fluxbuf[...]
    fcopy = remote(fluxbuf, flux_in, hsend.at[8], hrecv.at[8], (west, sub))
    fcopy.start()
    for cp in ocean_copies[1:]:
        cp.wait()
    fcopy.wait()

    blocks = jnp.concatenate(
        [fluxbuf[:, g * LANES : (g + 1) * LANES] for g in range(groups)]
        + [flux_in[:, g * LANES : (g + 1) * LANES] for g in range(groups)],
        axis=0,
    )
    for k in range(width):
        src = ids_ocean[:, k : k + 1]
        grp = jnp.remainder(src % ngroups - lon * groups, ngroups)
        ids = grp * aband + (src // ngroups - sub * aband)
        apicked[k] = dot(one_hot(ids, 2 * groups * aband), blocks)
    wa = ids_ocean[:, width:]

    def a2o_step(w, acc):
        part = jnp.where(wa[:, 0:1] == w, apicked[0], 0.0)
        for k in range(1, width):
            part = part + jnp.where(wa[:, k : k + 1] == w, apicked[k], 0.0)
        return acc + dot_nt(part, wbuf[w])

    flux_ocean = lax.fori_loop(
        0, nw, a2o_step, jnp.zeros((orows, LANES), jnp.float32), unroll=4
    )

    rev_r = lax.broadcasted_iota(jnp.int32, (LANES, LANES), 0)
    rev_c = lax.broadcasted_iota(jnp.int32, (LANES, LANES), 1)
    rev = jnp.where(rev_r + rev_c == LANES - 1, 1.0, 0.0).astype(jnp.float32)
    folded = dot(edge_in[2], rev)
    s_row = jnp.where(sub == 0, edge[0], edge_in[0])
    n_row = jnp.where(sub == n_sub - 1, folded, edge_in[1])
    edge[0] = s_row
    edge[1] = n_row
    olane = lax.broadcasted_iota(jnp.int32, (orows, LANES), 1)
    orow = lax.broadcasted_iota(jnp.int32, (orows, LANES), 0)
    diff = diff_ref[...]

    def step(l, carry):
        x = ocean_ref[l]
        ow = jnp.where(olane == 0, pltpu.roll(tile_in[0, l], 1, 1), pltpu.roll(x, 1, 1))
        oe = jnp.where(
            olane == LANES - 1,
            pltpu.roll(tile_in[1, l], LANES - 1, 1),
            pltpu.roll(x, LANES - 1, 1),
        )
        so = jnp.where(orow == 0, edge[0, pl.ds(l, 1), :], pltpu.roll(x, 1, 0))
        no = jnp.where(orow == orows - 1, edge[1, pl.ds(l, 1), :], pltpu.roll(x, orows - 1, 0))
        lap = ow + oe + no + so - 4.0 * x
        otmp[l] = maskf * (x + diff * lap)
        return carry

    lax.fori_loop(0, olev, step, 0, unroll=2)
    otmp[0] = otmp[0] + maskf * flux_ocean
    stepped = jnp.swapaxes(otmp[...], 0, 1)
    for r in range(orows):
        otmp2[r] = dot(oinv_ref[...], stepped[r])
    onew_ref[...] = jnp.swapaxes(otmp2[...], 0, 1)

    for cp in sends2:
        cp.wait()


def write_out(air, ocean, flux, air_out, ocean_out, flux_out, sem):
    step = air.shape[0] // WRITES
    copies = [
        pltpu.make_async_copy(
            air.at[pl.ds(i * step, step)], air_out.at[pl.ds(i * step, step)], sem.at[i]
        )
        for i in range(WRITES)
    ]
    copies.append(pltpu.make_async_copy(ocean, ocean_out, sem.at[WRITES]))
    copies.append(pltpu.make_async_copy(flux, flux_out, sem.at[WRITES + 1]))
    for cp in copies:
        cp.start()
    for cp in copies:
        cp.wait()


def per_device(
    atm_tracer,
    courant,
    column_inverse,
    heat_exchange_factor,
    ocean_temp,
    diffusivity,
    ocean_inverse,
    land_mask,
    regrid_weight_blocks,
    a2o_src,
    a2o_wgt,
    o2a_src,
    o2a_wgt,
):
    n_lon = lax.axis_size("lon")
    n_sub = lax.axis_size("sub")
    lev_dev, alat, alon = atm_tracer.shape
    levels = lev_dev * n_sub
    aband = alat // n_sub
    nchunk = aband // ROWS
    local_bands = column_inverse.shape[0] // n_sub
    olev, orows, olon = ocean_temp.shape
    groups = alon // LANES
    width = a2o_src.shape[2]
    f32 = jnp.float32
    vm = pl.BlockSpec(memory_space=pltpu.VMEM)
    hbm = pl.BlockSpec(memory_space=pltpu.HBM)
    anywhere = pl.BlockSpec(memory_space=pl.ANY)
    results = pl.pallas_call(
        functools.partial(kernel, n_lon, n_sub),
        out_shape=(
            pltpu.VMEM(atm_tracer.shape, f32),
            pltpu.VMEM(ocean_temp.shape, f32),
            pltpu.VMEM((aband, alon), f32),
        ),
        in_specs=[hbm] * 13,
        out_specs=(anywhere, vm, vm),
        scratch_shapes=[
            pltpu.VMEM((lev_dev, n_sub, aband, alon), f32),
            pltpu.VMEM((lev_dev, n_sub, aband, alon), f32),
            pltpu.VMEM((lev_dev, n_sub, aband, alon), f32),
            pltpu.VMEM((levels, aband, alon), f32),
            pltpu.VMEM((levels, aband, alon), f32),
            pltpu.VMEM((ROWS, levels, alon), f32),
            pltpu.VMEM((ROWS, levels, alon), f32),
            pltpu.VMEM(regrid_weight_blocks.shape, f32),
            pltpu.VMEM((local_bands, levels, levels), f32),
            pltpu.VMEM((aband, alon), f32),
            pltpu.VMEM(ocean_temp.shape, f32),
            pltpu.VMEM(diffusivity.shape, f32),
            pltpu.VMEM(ocean_inverse.shape, f32),
            pltpu.VMEM(land_mask.shape, jnp.int32),
            pltpu.VMEM((1, width, orows), jnp.int32),
            pltpu.VMEM((1, width, orows), jnp.int32),
            pltpu.VMEM((groups, width, alat), jnp.int32),
            pltpu.VMEM((groups, width, alat), jnp.int32),
            pltpu.VMEM((groups, alat, 2 * width), jnp.int32),
            pltpu.VMEM((2 * width, LANES), jnp.int32),
            pltpu.VMEM((2, nchunk, n_sub, ROWS, LANES), f32),
            pltpu.VMEM((2, nchunk, n_sub, ROWS, LANES), f32),
            pltpu.VMEM((n_sub, 2, ROWS, LANES), f32),
            pltpu.VMEM((n_sub, 2, ROWS, LANES), f32),
            pltpu.VMEM((2, orows, olon), f32),
            pltpu.VMEM((2, olev, orows, olon), f32),
            pltpu.VMEM((2, olev, olon), f32),
            pltpu.VMEM((3, olev, olon), f32),
            pltpu.VMEM((aband, alon), f32),
            pltpu.VMEM((aband, alon), f32),
            pltpu.VMEM((width, groups * aband, LANES), f32),
            pltpu.VMEM((width, orows, LANES), f32),
            pltpu.VMEM((aband, alon), f32),
            pltpu.VMEM((olev, orows, olon), f32),
            pltpu.VMEM((orows, olev, olon), f32),
            pltpu.SemaphoreType.DMA((11,)),
            pltpu.SemaphoreType.DMA((2, nchunk)),
            pltpu.SemaphoreType.DMA((nchunk,)),
            pltpu.SemaphoreType.DMA((2, nchunk)),
            pltpu.SemaphoreType.DMA((2, nchunk)),
            pltpu.SemaphoreType.DMA((n_sub,)),
            pltpu.SemaphoreType.DMA((n_sub,)),
            pltpu.SemaphoreType.DMA((nchunk, n_sub)),
            pltpu.SemaphoreType.DMA((nchunk, n_sub)),
            pltpu.SemaphoreType.DMA((nchunk, n_sub)),
            pltpu.SemaphoreType.DMA((nchunk, n_sub)),
            pltpu.SemaphoreType.DMA((9,)),
            pltpu.SemaphoreType.DMA((9,)),
        ],
        compiler_params=pltpu.CompilerParams(
            collective_id=0, has_side_effects=True, vmem_limit_bytes=48 * 1024 * 1024
        ),
        name="step",
    )(*(pltpu.with_memory_space_constraint(v, pltpu.HBM) for v in (
        atm_tracer.reshape(lev_dev, n_sub, aband, alon),
        courant.reshape(lev_dev, n_sub, aband, alon),
        column_inverse,
        heat_exchange_factor,
        ocean_temp,
        diffusivity,
        ocean_inverse,
        land_mask,
        regrid_weight_blocks,
        jnp.transpose(a2o_src, (1, 2, 0)),
        jnp.transpose(a2o_wgt, (1, 2, 0)),
        jnp.transpose(o2a_src, (1, 2, 0)),
        jnp.transpose(o2a_wgt, (1, 2, 0)),
    )))
    return pl.pallas_call(
        write_out,
        out_shape=[jax.ShapeDtypeStruct(v.shape, f32) for v in results],
        in_specs=[anywhere] * 3,
        out_specs=[hbm] * 3,
        scratch_shapes=[pltpu.SemaphoreType.DMA((WRITES + 2,))],
        compiler_params=pltpu.CompilerParams(vmem_limit_bytes=1024 * 1024),
        name="write_out",
    )(*results)


def solution(mesh):
    return jax.shard_map(
        per_device,
        mesh=mesh,
        in_specs=(
            P("sub", None, "lon"),
            P("sub", None, "lon"),
            P(),
            P(None, "lon"),
            P(None, "sub", "lon"),
            P("sub", "lon"),
            P(),
            P("sub", "lon"),
            P(),
            P("sub", "lon", None),
            P("sub", "lon", None),
            P(None, "lon", None),
            P(None, "lon", None),
        ),
        out_specs=(P("sub", None, "lon"), P(None, "sub", "lon"), P("sub", "lon")),
        check_vma=False,
    )
```

```python
import functools

import jax
import jax.numpy as jnp
from jax import lax
from jax.experimental import pallas as pl
from jax.experimental.pallas import tpu as pltpu
from jax.sharding import PartitionSpec as P

HI = lax.Precision.HIGHEST
MESH = pl.DeviceIdType.MESH
ROWS = 8
LANES = 128
WRITES = 4


def dot(a, b):
    return jnp.dot(a, b, precision=HI, preferred_element_type=jnp.float32)


def dot_nt(a, b):
    return lax.dot_general(
        a, b, (((1,), (1,)), ((), ())), precision=HI, preferred_element_type=jnp.float32
    )


def one_hot(ids, count):
    cols = lax.broadcasted_iota(jnp.int32, (ids.shape[0], count), 1)
    return jnp.where(cols == ids, 1.0, 0.0).astype(jnp.float32)


def kernel(
    n_lon,
    n_sub,
    atm_hbm,
    cour_hbm,
    colinv_hbm,
    heat_hbm,
    ocean_hbm,
    diff_hbm,
    oinv_hbm,
    mask_hbm,
    w_hbm,
    a2o_src_hbm,
    a2o_wgt_hbm,
    o2a_src_hbm,
    o2a_wgt_hbm,
    out_ref,
    onew_ref,
    flux_ref,
    xbuf,
    cbuf,
    adv,
    cols,
    res,
    tmp,
    tmp2,
    wbuf,
    inv,
    heat_ref,
    ocean_ref,
    diff_ref,
    oinv_ref,
    mask_ref,
    a2o_src_ref,
    a2o_wgt_ref,
    o2a_src_ref,
    o2a_wgt_ref,
    ids_a,
    ids_o,
    halo,
    halo_in,
    corr,
    corr_in,
    sea,
    tile_in,
    edge,
    edge_in,
    fluxbuf,
    flux_in,
    picked,
    apicked,
    sst,
    otmp,
    otmp2,
    local_sem,
    load_sem,
    own_sem,
    xsend,
    xrecv,
    csend,
    crecv,
    send1,
    recv1,
    send2,
    recv2,
    hsend,
    hrecv,
):
    lon = lax.axis_index("lon")
    sub = lax.axis_index("sub")
    lev_dev, _, aband, alon = xbuf.shape
    levels = lev_dev * n_sub
    nchunk = aband // ROWS
    local_bands = inv.shape[0]
    rows_band = aband // local_bands
    groups = alon // LANES
    ngroups = groups * n_lon
    olev, orows, _ = ocean_ref.shape
    nw = wbuf.shape[0]
    width = a2o_src_ref.shape[1]

    east = lax.rem(lon + 1, n_lon)
    west = lax.rem(lon + n_lon - 1, n_lon)
    mirror = n_lon - 1 - lon
    north = lax.rem(sub + 1, n_sub)
    south = lax.rem(sub + n_sub - 1, n_sub)

    load_x = []
    load_c = []
    for t in range(nchunk):
        part = pl.ds(t * ROWS, ROWS)
        for hbm, buf, loads, i in ((atm_hbm, xbuf, load_x, 0), (cour_hbm, cbuf, load_c, 1)):
            cp = pltpu.make_async_copy(
                hbm.at[:, :, part, :], buf.at[:, :, part, :], load_sem.at[i, t]
            )
            if t == 0:
                cp.start()
            loads.append(cp)
    small = [
        pltpu.make_async_copy(hbm, buf, local_sem.at[i])
        for i, (hbm, buf) in enumerate(
            (
                (ocean_hbm, ocean_ref),
                (mask_hbm, mask_ref),
                (colinv_hbm.at[pl.ds(sub * local_bands, local_bands)], inv),
                (heat_hbm.at[pl.ds(sub * aband, aband)], heat_ref),
                (diff_hbm, diff_ref),
                (oinv_hbm, oinv_ref),
                (a2o_src_hbm, a2o_src_ref),
                (a2o_wgt_hbm, a2o_wgt_ref),
                (o2a_src_hbm, o2a_src_ref),
                (o2a_wgt_hbm, o2a_wgt_ref),
                (w_hbm, wbuf),
            )
        )
    ]
    barrier = pltpu.get_barrier_semaphore()
    for target in (east, west, mirror):
        pl.semaphore_signal(barrier, inc=1, device_id=(target, sub), device_id_type=MESH)
    for off in range(1, n_sub):
        peer = lax.rem(sub + off, n_sub)
        pl.semaphore_signal(barrier, inc=1, device_id=(lon, peer), device_id_type=MESH)

    def remote(src, dst, ssem, rsem, target):
        return pltpu.make_async_remote_copy(
            src_ref=src, dst_ref=dst, send_sem=ssem, recv_sem=rsem,
            device_id=target, device_id_type=MESH,
        )

    lane = lax.broadcasted_iota(jnp.int32, (n_sub, ROWS, LANES), 2)

    def pack(buf, t):
        rows = slice(t * ROWS, (t + 1) * ROWS)

        def body(l, carry):
            tail, head = carry
            last = buf[l, :, rows, alon - LANES :]
            first = buf[l, :, rows, :LANES]
            tail = jnp.where(lane == l, pltpu.roll(last, lax.rem(l + 1, LANES), 2), tail)
            head = jnp.where(lane == l, pltpu.roll(first, l, 2), head)
            return tail, head

        zero = jnp.zeros((n_sub, ROWS, LANES), jnp.float32)
        return lax.fori_loop(0, lev_dev, body, (zero, zero), unroll=8)

    def halo_copies(t):
        tail, head = pack(xbuf, t)
        halo[0, t] = tail
        halo[1, t] = head
        pair = [
            remote(halo.at[i, t], halo_in.at[i, t], xsend.at[i, t], xrecv.at[i, t], (side, sub))
            for i, side in ((0, east), (1, west))
        ]
        for cp in pair:
            cp.start()
        return pair

    wide = lax.broadcasted_iota(jnp.int32, (ROWS, alon), 1)

    def advect(d, t, write):
        rows = slice(t * ROWS, (t + 1) * ROWS)

        def body(l, carry):
            x = xbuf[l, d, rows, :]
            c = cbuf[l, d, rows, :]
            if t == 0:
                edges = 0.0
            else:
                hw = pltpu.roll(halo_in[0, t, d], lax.rem(LANES - l, LANES), 1)
                he = pltpu.roll(halo_in[1, t, d], LANES - 1 - l, 1)
                edges = jnp.concatenate([hw] * (groups - 1) + [he], axis=1)
            xw = jnp.where(wide == 0, edges, pltpu.roll(x, 1, 1))
            xe = jnp.where(wide == alon - 1, edges, pltpu.roll(x, alon - 1, 1))
            write(l, x - jnp.maximum(c, 0.0) * (x - xw) - jnp.minimum(c, 0.0) * (xe - x))
            return carry

        lax.fori_loop(0, lev_dev, body, 0, unroll=8)

    offs = [n_sub // 2] + [o for o in range(n_sub - 1, 0, -1) if o != n_sub // 2]
    sends1 = []

    def advect_to(off, t):
        peer = lax.rem(sub + off, n_sub)
        rows = slice(t * ROWS, (t + 1) * ROWS)

        def keep(l, value):
            adv[l, peer, rows, :] = value

        advect(peer, t, keep)

    def send_to(off, t):
        peer = lax.rem(sub + off, n_sub)
        cp = remote(
            adv.at[:, peer, pl.ds(t * ROWS, ROWS), :],
            cols.at[pl.ds(sub * lev_dev, lev_dev), pl.ds(t * ROWS, ROWS), :],
            send1.at[t, off],
            recv1.at[t, off],
            (lon, peer),
        )
        cp.start()
        sends1.append((t, cp))

    def advect_own(t):
        rows = slice(t * ROWS, (t + 1) * ROWS)

        def keep(l, value):
            cols[sub * lev_dev + l, rows, :] = value

        advect(sub, t, keep)

    load_x[0].wait()
    load_c[0].wait()
    for cp in load_x[1:] + load_c[1:] + small:
        cp.start()
    advect_to(offs[0], 0)
    pl.semaphore_wait(barrier, 3 + n_sub - 1)
    send_to(offs[0], 0)
    for off in offs[1:]:
        advect_to(off, 0)
        send_to(off, 0)
    halos = [halo_copies(0)]
    for t in range(1, nchunk):
        load_x[t].wait()
        halos.append(halo_copies(t))
    advect_own(0)
    ctail, chead = pack(cbuf, 0)
    for cp in halos[0]:
        cp.wait()
    share_west = jnp.maximum(chead, 0.0) * halo_in[0, 0]
    share_east = -jnp.minimum(ctail, 0.0) * halo_in[1, 0]
    corr[...] = share_west + pltpu.roll(share_east, lev_dev, 2)
    shares = []
    for off in offs:
        peer = lax.rem(sub + off, n_sub)
        cp = remote(
            corr.at[peer], corr_in.at[sub], csend.at[off], crecv.at[off], (lon, peer)
        )
        cp.start()
        shares.append(cp)
    corr_in[sub] = corr[sub]
    for t in range(1, nchunk):
        load_c[t].wait()
        for cp in halos[t]:
            cp.wait()
        for off in offs:
            advect_to(off, t)
            send_to(off, t)
        advect_own(t)

    for cp in small[:2]:
        cp.wait()
    maskf = mask_ref[...].astype(jnp.float32)
    sea[0] = maskf * ocean_ref[0]
    edge[0] = ocean_ref[:, 0, :]
    edge[1] = ocean_ref[:, orows - 1, :]
    ocean_copies = [
        remote(sea.at[0], sea.at[1], hsend.at[2], hrecv.at[2], (east, sub)),
        remote(ocean_ref, tile_in.at[0], hsend.at[3], hrecv.at[3], (east, sub)),
        remote(ocean_ref, tile_in.at[1], hsend.at[4], hrecv.at[4], (west, sub)),
        remote(edge.at[1], edge_in.at[2], hsend.at[7], hrecv.at[7], (mirror, sub)),
    ]
    for cp in ocean_copies:
        cp.start()
    to_north = remote(edge.at[1], edge_in.at[0], hsend.at[5], hrecv.at[5], (lon, north))
    to_south = remote(edge.at[0], edge_in.at[1], hsend.at[6], hrecv.at[6], (lon, south))

    @pl.when(sub < n_sub - 1)
    def _():
        to_north.start()

    @pl.when(sub > 0)
    def _():
        to_south.start()

    for cp in small[2:]:
        cp.wait()
    for g in range(groups):
        pair = jnp.concatenate([o2a_src_ref[g], o2a_wgt_ref[g]], axis=0)
        ids_a[g] = jnp.transpose(pair, (1, 0))
    ids_o[...] = jnp.zeros_like(ids_o)
    ids_o[:width, :orows] = a2o_src_ref[0]
    ids_o[width : 2 * width, :orows] = a2o_wgt_ref[0]
    ids_ocean = jnp.transpose(ids_o[...], (1, 0))[:orows]

    ocean_copies[0].wait()
    window = jnp.concatenate([sea[1], sea[0]], axis=0)
    band = pl.ds(sub * aband, aband)
    for g in range(groups):
        for k in range(width):
            src = ids_a[g, band, :][:, k : k + 1]
            tile = jnp.remainder(src % n_lon - lon + 1, n_lon)
            ids = tile * orows + (src // n_lon - sub * orows)
            picked[k, g * aband : (g + 1) * aband, :] = dot(one_hot(ids, 2 * orows), window)
    wg = jnp.concatenate([ids_a[g, band, :][:, width:] for g in range(groups)], axis=0)

    def sst_step(w, acc):
        part = jnp.where(wg[:, 0:1] == w, picked[0], 0.0)
        for k in range(1, width):
            part = part + jnp.where(wg[:, k : k + 1] == w, picked[k], 0.0)
        return acc + dot_nt(part, wbuf[w])

    acc = lax.fori_loop(
        0, nw, sst_step, jnp.zeros((groups * aband, LANES), jnp.float32), unroll=2
    )
    for g in range(groups):
        sst[:, g * LANES : (g + 1) * LANES] = acc[g * aband : (g + 1) * aband]

    sends2 = []
    for t in range(nchunk):
        for tt, cp in sends1:
            if tt == t:
                cp.wait()
        if t == 0:
            for cp in shares:
                cp.wait()
            for s in range(n_sub):

                def add_share(l, carry, s=s):
                    w = pltpu.roll(corr_in[s], lax.rem(LANES - l, LANES), 1)
                    e = pltpu.roll(corr_in[s], LANES - 1 - l - lev_dev, 1)
                    both = jnp.concatenate([w] * (groups - 1) + [e], axis=1)
                    ends = (wide == 0) | (wide == alon - 1)
                    old = cols[s * lev_dev + l, :ROWS, :]
                    cols[s * lev_dev + l, :ROWS, :] = old + jnp.where(ends, both, 0.0)
                    return carry

                lax.fori_loop(0, lev_dev, add_share, 0, unroll=4)
        rows = slice(t * ROWS, (t + 1) * ROWS)

        def turn(i, carry, rows=rows):
            part = cols[pl.ds(i * ROWS, ROWS), rows, :]
            tmp[:, pl.ds(i * ROWS, ROWS), :] = jnp.swapaxes(part, 0, 1)
            return carry

        lax.fori_loop(0, levels // ROWS, turn, 0, unroll=2)

        def solve(r, carry, t=t):
            tmp2[r] = dot(inv[t * ROWS // rows_band], tmp[r])
            return carry

        lax.fori_loop(0, ROWS, solve, 0)

        def back(i, carry, rows=rows):
            part = tmp2[:, pl.ds(i * ROWS, ROWS), :]
            res[pl.ds(i * ROWS, ROWS), rows, :] = jnp.swapaxes(part, 0, 1)
            return carry

        lax.fori_loop(0, levels // ROWS, back, 0, unroll=2)
        for off in offs:
            peer = lax.rem(sub + off, n_sub)
            cp = remote(
                res.at[pl.ds(peer * lev_dev, lev_dev), pl.ds(t * ROWS, ROWS), :],
                out_ref.at[:, pl.ds(sub * aband + t * ROWS, ROWS), :],
                send2.at[t, off],
                recv2.at[t, off],
                (lon, peer),
            )
            cp.start()
            sends2.append(cp)
        own = pltpu.make_async_copy(
            res.at[pl.ds(sub * lev_dev, lev_dev), pl.ds(t * ROWS, ROWS), :],
            out_ref.at[:, pl.ds(sub * aband + t * ROWS, ROWS), :],
            own_sem.at[t],
        )
        own.start()
        sends2.append(own)

    fluxbuf[...] = heat_ref[...] * (sst[...] - res[levels - 1])
    flux_ref[...] = fluxbuf[...]
    fcopy = remote(fluxbuf, flux_in, hsend.at[8], hrecv.at[8], (west, sub))
    fcopy.start()
    for cp in ocean_copies[1:]:
        cp.wait()

    @pl.when(sub < n_sub - 1)
    def _():
        to_north.wait_send()
        to_south.wait_recv()

    @pl.when(sub > 0)
    def _():
        to_south.wait_send()
        to_north.wait_recv()

    fcopy.wait()

    blocks = jnp.concatenate(
        [fluxbuf[:, g * LANES : (g + 1) * LANES] for g in range(groups)]
        + [flux_in[:, g * LANES : (g + 1) * LANES] for g in range(groups)],
        axis=0,
    )
    for k in range(width):
        src = ids_ocean[:, k : k + 1]
        grp = jnp.remainder(src % ngroups - lon * groups, ngroups)
        ids = grp * aband + (src // ngroups - sub * aband)
        apicked[k] = dot(one_hot(ids, 2 * groups * aband), blocks)
    wa = ids_ocean[:, width:]

    def a2o_step(w, acc):
        part = jnp.where(wa[:, 0:1] == w, apicked[0], 0.0)
        for k in range(1, width):
            part = part + jnp.where(wa[:, k : k + 1] == w, apicked[k], 0.0)
        return acc + dot_nt(part, wbuf[w])

    flux_ocean = lax.fori_loop(
        0, nw, a2o_step, jnp.zeros((orows, LANES), jnp.float32), unroll=4
    )

    rev_r = lax.broadcasted_iota(jnp.int32, (LANES, LANES), 0)
    rev_c = lax.broadcasted_iota(jnp.int32, (LANES, LANES), 1)
    rev = jnp.where(rev_r + rev_c == LANES - 1, 1.0, 0.0).astype(jnp.float32)
    folded = dot(edge_in[2], rev)

    @pl.when(sub > 0)
    def _():
        edge[0] = edge_in[0]

    edge[1] = folded

    @pl.when(sub < n_sub - 1)
    def _():
        edge[1] = edge_in[1]

    olane = lax.broadcasted_iota(jnp.int32, (orows, LANES), 1)
    orow = lax.broadcasted_iota(jnp.int32, (orows, LANES), 0)
    diff = diff_ref[...]

    def step(l, carry):
        x = ocean_ref[l]
        ow = jnp.where(olane == 0, pltpu.roll(tile_in[0, l], 1, 1), pltpu.roll(x, 1, 1))
        oe = jnp.where(
            olane == LANES - 1,
            pltpu.roll(tile_in[1, l], LANES - 1, 1),
            pltpu.roll(x, LANES - 1, 1),
        )
        so = jnp.where(orow == 0, edge[0, pl.ds(l, 1), :], pltpu.roll(x, 1, 0))
        no = jnp.where(orow == orows - 1, edge[1, pl.ds(l, 1), :], pltpu.roll(x, orows - 1, 0))
        lap = ow + oe + no + so - 4.0 * x
        otmp[l] = maskf * (x + diff * lap)
        return carry

    lax.fori_loop(0, olev, step, 0, unroll=2)
    otmp[0] = otmp[0] + maskf * flux_ocean
    stepped = jnp.swapaxes(otmp[...], 0, 1)
    for r in range(orows):
        otmp2[r] = dot(oinv_ref[...], stepped[r])
    onew_ref[...] = jnp.swapaxes(otmp2[...], 0, 1)

    for cp in sends2:
        cp.wait()


def write_out(air, ocean, flux, air_out, ocean_out, flux_out, sem):
    step = air.shape[0] // WRITES
    copies = [
        pltpu.make_async_copy(
            air.at[pl.ds(i * step, step)], air_out.at[pl.ds(i * step, step)], sem.at[i]
        )
        for i in range(WRITES)
    ]
    copies.append(pltpu.make_async_copy(ocean, ocean_out, sem.at[WRITES]))
    copies.append(pltpu.make_async_copy(flux, flux_out, sem.at[WRITES + 1]))
    for cp in copies:
        cp.start()
    for cp in copies:
        cp.wait()


def per_device(
    atm_tracer,
    courant,
    column_inverse,
    heat_exchange_factor,
    ocean_temp,
    diffusivity,
    ocean_inverse,
    land_mask,
    regrid_weight_blocks,
    a2o_src,
    a2o_wgt,
    o2a_src,
    o2a_wgt,
):
    n_lon = lax.axis_size("lon")
    n_sub = lax.axis_size("sub")
    lev_dev, alat, alon = atm_tracer.shape
    levels = lev_dev * n_sub
    aband = alat // n_sub
    nchunk = aband // ROWS
    local_bands = column_inverse.shape[0] // n_sub
    olev, orows, olon = ocean_temp.shape
    groups = alon // LANES
    width = a2o_src.shape[2]
    f32 = jnp.float32
    vm = pl.BlockSpec(memory_space=pltpu.VMEM)
    hbm = pl.BlockSpec(memory_space=pltpu.HBM)
    anywhere = pl.BlockSpec(memory_space=pl.ANY)
    results = pl.pallas_call(
        functools.partial(kernel, n_lon, n_sub),
        out_shape=(
            pltpu.VMEM(atm_tracer.shape, f32),
            pltpu.VMEM(ocean_temp.shape, f32),
            pltpu.VMEM((aband, alon), f32),
        ),
        in_specs=[hbm] * 13,
        out_specs=(anywhere, vm, vm),
        scratch_shapes=[
            pltpu.VMEM((lev_dev, n_sub, aband, alon), f32),
            pltpu.VMEM((lev_dev, n_sub, aband, alon), f32),
            pltpu.VMEM((lev_dev, n_sub, aband, alon), f32),
            pltpu.VMEM((levels, aband, alon), f32),
            pltpu.VMEM((levels, aband, alon), f32),
            pltpu.VMEM((ROWS, levels, alon), f32),
            pltpu.VMEM((ROWS, levels, alon), f32),
            pltpu.VMEM(regrid_weight_blocks.shape, f32),
            pltpu.VMEM((local_bands, levels, levels), f32),
            pltpu.VMEM((aband, alon), f32),
            pltpu.VMEM(ocean_temp.shape, f32),
            pltpu.VMEM(diffusivity.shape, f32),
            pltpu.VMEM(ocean_inverse.shape, f32),
            pltpu.VMEM(land_mask.shape, jnp.int32),
            pltpu.VMEM((1, width, orows), jnp.int32),
            pltpu.VMEM((1, width, orows), jnp.int32),
            pltpu.VMEM((groups, width, alat), jnp.int32),
            pltpu.VMEM((groups, width, alat), jnp.int32),
            pltpu.VMEM((groups, alat, 2 * width), jnp.int32),
            pltpu.VMEM((2 * width, LANES), jnp.int32),
            pltpu.VMEM((2, nchunk, n_sub, ROWS, LANES), f32),
            pltpu.VMEM((2, nchunk, n_sub, ROWS, LANES), f32),
            pltpu.VMEM((n_sub, ROWS, LANES), f32),
            pltpu.VMEM((n_sub, ROWS, LANES), f32),
            pltpu.VMEM((2, orows, olon), f32),
            pltpu.VMEM((2, olev, orows, olon), f32),
            pltpu.VMEM((2, olev, olon), f32),
            pltpu.VMEM((3, olev, olon), f32),
            pltpu.VMEM((aband, alon), f32),
            pltpu.VMEM((aband, alon), f32),
            pltpu.VMEM((width, groups * aband, LANES), f32),
            pltpu.VMEM((width, orows, LANES), f32),
            pltpu.VMEM((aband, alon), f32),
            pltpu.VMEM((olev, orows, olon), f32),
            pltpu.VMEM((orows, olev, olon), f32),
            pltpu.SemaphoreType.DMA((11,)),
            pltpu.SemaphoreType.DMA((2, nchunk)),
            pltpu.SemaphoreType.DMA((nchunk,)),
            pltpu.SemaphoreType.DMA((2, nchunk)),
            pltpu.SemaphoreType.DMA((2, nchunk)),
            pltpu.SemaphoreType.DMA((n_sub,)),
            pltpu.SemaphoreType.DMA((n_sub,)),
            pltpu.SemaphoreType.DMA((nchunk, n_sub)),
            pltpu.SemaphoreType.DMA((nchunk, n_sub)),
            pltpu.SemaphoreType.DMA((nchunk, n_sub)),
            pltpu.SemaphoreType.DMA((nchunk, n_sub)),
            pltpu.SemaphoreType.DMA((9,)),
            pltpu.SemaphoreType.DMA((9,)),
        ],
        compiler_params=pltpu.CompilerParams(
            collective_id=0, has_side_effects=True, vmem_limit_bytes=48 * 1024 * 1024
        ),
        name="step",
    )(*(pltpu.with_memory_space_constraint(v, pltpu.HBM) for v in (
        atm_tracer.reshape(lev_dev, n_sub, aband, alon),
        courant.reshape(lev_dev, n_sub, aband, alon),
        column_inverse,
        heat_exchange_factor,
        ocean_temp,
        diffusivity,
        ocean_inverse,
        land_mask,
        regrid_weight_blocks,
        jnp.transpose(a2o_src, (1, 2, 0)),
        jnp.transpose(a2o_wgt, (1, 2, 0)),
        jnp.transpose(o2a_src, (1, 2, 0)),
        jnp.transpose(o2a_wgt, (1, 2, 0)),
    )))
    return pl.pallas_call(
        write_out,
        out_shape=[jax.ShapeDtypeStruct(v.shape, f32) for v in results],
        in_specs=[anywhere] * 3,
        out_specs=[hbm] * 3,
        scratch_shapes=[pltpu.SemaphoreType.DMA((WRITES + 2,))],
        compiler_params=pltpu.CompilerParams(vmem_limit_bytes=1024 * 1024),
        name="write_out",
    )(*results)


def solution(mesh):
    return jax.shard_map(
        per_device,
        mesh=mesh,
        in_specs=(
            P("sub", None, "lon"),
            P("sub", None, "lon"),
            P(),
            P(None, "lon"),
            P(None, "sub", "lon"),
            P("sub", "lon"),
            P(),
            P("sub", "lon"),
            P(),
            P("sub", "lon", None),
            P("sub", "lon", None),
            P(None, "lon", None),
            P(None, "lon", None),
        ),
        out_specs=(P("sub", None, "lon"), P(None, "sub", "lon"), P("sub", "lon")),
        check_vma=False,
    )
```

```python
import functools

import jax
import jax.numpy as jnp
from jax import lax
from jax.experimental import pallas as pl
from jax.experimental.pallas import tpu as pltpu
from jax.sharding import PartitionSpec as P

HI = lax.Precision.HIGHEST
MESH = pl.DeviceIdType.MESH
ROWS = 8
LANES = 128
WRITES = 4


def dot(a, b):
    return jnp.dot(a, b, precision=HI, preferred_element_type=jnp.float32)


def dot_nt(a, b):
    return lax.dot_general(
        a, b, (((1,), (1,)), ((), ())), precision=HI, preferred_element_type=jnp.float32
    )


def one_hot(ids, count):
    cols = lax.broadcasted_iota(jnp.int32, (ids.shape[0], count), 1)
    return jnp.where(cols == ids, 1.0, 0.0).astype(jnp.float32)


def kernel(
    n_lon,
    n_sub,
    atm_hbm,
    cour_hbm,
    colinv_hbm,
    heat_hbm,
    ocean_hbm,
    diff_hbm,
    oinv_hbm,
    mask_hbm,
    w_hbm,
    a2o_src_hbm,
    a2o_wgt_hbm,
    o2a_src_hbm,
    o2a_wgt_hbm,
    out_ref,
    onew_ref,
    flux_ref,
    xbuf,
    cbuf,
    adv,
    cols,
    res,
    tmp,
    tmp2,
    wbuf,
    inv,
    heat_ref,
    ocean_ref,
    diff_ref,
    oinv_ref,
    mask_ref,
    a2o_src_ref,
    a2o_wgt_ref,
    o2a_src_ref,
    o2a_wgt_ref,
    ids_a,
    ids_o,
    halo,
    halo_in,
    corr,
    corr_in,
    sea,
    tile_in,
    edge,
    edge_in,
    fluxbuf,
    flux_in,
    picked,
    apicked,
    sst,
    otmp,
    otmp2,
    local_sem,
    load_sem,
    own_sem,
    xsend,
    xrecv,
    csend,
    crecv,
    send1,
    recv1,
    send2,
    recv2,
    hsend,
    hrecv,
):
    lon = lax.axis_index("lon")
    sub = lax.axis_index("sub")
    lev_dev, _, aband, alon = xbuf.shape
    levels = lev_dev * n_sub
    nchunk = aband // ROWS
    local_bands = inv.shape[0]
    rows_band = aband // local_bands
    groups = alon // LANES
    ngroups = groups * n_lon
    olev, orows, _ = ocean_ref.shape
    nw = wbuf.shape[0]
    width = a2o_src_ref.shape[1]

    east = lax.rem(lon + 1, n_lon)
    west = lax.rem(lon + n_lon - 1, n_lon)
    mirror = n_lon - 1 - lon
    north = lax.rem(sub + 1, n_sub)
    south = lax.rem(sub + n_sub - 1, n_sub)

    load_x = []
    load_c = []
    for t in range(nchunk):
        part = pl.ds(t * ROWS, ROWS)
        for hbm, buf, loads, i in ((atm_hbm, xbuf, load_x, 0), (cour_hbm, cbuf, load_c, 1)):
            cp = pltpu.make_async_copy(
                hbm.at[:, :, part, :], buf.at[:, :, part, :], load_sem.at[i, t]
            )
            if t == 0:
                cp.start()
            loads.append(cp)
    small = [
        pltpu.make_async_copy(hbm, buf, local_sem.at[i])
        for i, (hbm, buf) in enumerate(
            (
                (ocean_hbm, ocean_ref),
                (mask_hbm, mask_ref),
                (colinv_hbm.at[pl.ds(sub * local_bands, local_bands)], inv),
                (heat_hbm.at[pl.ds(sub * aband, aband)], heat_ref),
                (diff_hbm, diff_ref),
                (oinv_hbm, oinv_ref),
                (a2o_src_hbm, a2o_src_ref),
                (a2o_wgt_hbm, a2o_wgt_ref),
                (o2a_src_hbm, o2a_src_ref),
                (o2a_wgt_hbm, o2a_wgt_ref),
                (w_hbm, wbuf),
            )
        )
    ]
    barrier = pltpu.get_barrier_semaphore()
    for target in (east, west, mirror):
        pl.semaphore_signal(barrier, inc=1, device_id=(target, sub), device_id_type=MESH)
    for off in range(1, n_sub):
        peer = lax.rem(sub + off, n_sub)
        pl.semaphore_signal(barrier, inc=1, device_id=(lon, peer), device_id_type=MESH)

    def remote(src, dst, ssem, rsem, target):
        return pltpu.make_async_remote_copy(
            src_ref=src, dst_ref=dst, send_sem=ssem, recv_sem=rsem,
            device_id=target, device_id_type=MESH,
        )

    lane = lax.broadcasted_iota(jnp.int32, (n_sub, ROWS, LANES), 2)

    def pack(buf, t):
        rows = slice(t * ROWS, (t + 1) * ROWS)

        def body(l, carry):
            tail, head = carry
            last = buf[l, :, rows, alon - LANES :]
            first = buf[l, :, rows, :LANES]
            tail = jnp.where(lane == l, pltpu.roll(last, lax.rem(l + 1, LANES), 2), tail)
            head = jnp.where(lane == l, pltpu.roll(first, l, 2), head)
            return tail, head

        zero = jnp.zeros((n_sub, ROWS, LANES), jnp.float32)
        return lax.fori_loop(0, lev_dev, body, (zero, zero), unroll=8)

    def halo_copies(t):
        tail, head = pack(xbuf, t)
        halo[0, t] = tail
        halo[1, t] = head
        pair = [
            remote(halo.at[i, t], halo_in.at[i, t], xsend.at[i, t], xrecv.at[i, t], (side, sub))
            for i, side in ((0, east), (1, west))
        ]
        for cp in pair:
            cp.start()
        return pair

    wide = lax.broadcasted_iota(jnp.int32, (ROWS, alon), 1)

    def advect(d, t, write):
        rows = slice(t * ROWS, (t + 1) * ROWS)

        def body(l, carry):
            x = xbuf[l, d, rows, :]
            c = cbuf[l, d, rows, :]
            if t == 0:
                edges = 0.0
            else:
                hw = pltpu.roll(halo_in[0, t, d], lax.rem(LANES - l, LANES), 1)
                he = pltpu.roll(halo_in[1, t, d], LANES - 1 - l, 1)
                edges = jnp.concatenate([hw] * (groups - 1) + [he], axis=1)
            xw = jnp.where(wide == 0, edges, pltpu.roll(x, 1, 1))
            xe = jnp.where(wide == alon - 1, edges, pltpu.roll(x, alon - 1, 1))
            write(l, x - jnp.maximum(c, 0.0) * (x - xw) - jnp.minimum(c, 0.0) * (xe - x))
            return carry

        lax.fori_loop(0, lev_dev, body, 0, unroll=8)

    offs = [n_sub // 2] + [o for o in range(n_sub - 1, 0, -1) if o != n_sub // 2]
    sends1 = []

    def advect_to(off, t):
        peer = lax.rem(sub + off, n_sub)

        def keep(l, value):
            adv[t, peer, l] = value

        advect(peer, t, keep)

    def send_to(off, t):
        peer = lax.rem(sub + off, n_sub)
        cp = remote(
            adv.at[t, peer],
            cols.at[t, pl.ds(sub * lev_dev, lev_dev)],
            send1.at[t, off],
            recv1.at[t, off],
            (lon, peer),
        )
        cp.start()
        sends1.append((t, cp))

    def advect_own(t):
        def keep(l, value):
            cols[t, sub * lev_dev + l] = value

        advect(sub, t, keep)

    load_x[0].wait()
    load_c[0].wait()
    for cp in load_x[1:] + load_c[1:] + small:
        cp.start()
    advect_to(offs[0], 0)
    pl.semaphore_wait(barrier, 3 + n_sub - 1)
    send_to(offs[0], 0)
    for off in offs[1:]:
        advect_to(off, 0)
        send_to(off, 0)
    halos = [halo_copies(0)]
    for t in range(1, nchunk):
        load_x[t].wait()
        halos.append(halo_copies(t))
    advect_own(0)
    ctail, chead = pack(cbuf, 0)
    for cp in halos[0]:
        cp.wait()
    share_west = jnp.maximum(chead, 0.0) * halo_in[0, 0]
    share_east = -jnp.minimum(ctail, 0.0) * halo_in[1, 0]
    corr[...] = share_west + pltpu.roll(share_east, lev_dev, 2)
    shares = []
    for off in offs:
        peer = lax.rem(sub + off, n_sub)
        cp = remote(
            corr.at[peer], corr_in.at[sub], csend.at[off], crecv.at[off], (lon, peer)
        )
        cp.start()
        shares.append(cp)
    corr_in[sub] = corr[sub]
    for t in range(1, nchunk):
        load_c[t].wait()
        for cp in halos[t]:
            cp.wait()
        for off in offs:
            advect_to(off, t)
            send_to(off, t)
        advect_own(t)

    for cp in small[:2]:
        cp.wait()
    maskf = mask_ref[...].astype(jnp.float32)
    sea[0] = maskf * ocean_ref[0]
    edge[0] = ocean_ref[:, 0, :]
    edge[1] = ocean_ref[:, orows - 1, :]
    ocean_copies = [
        remote(sea.at[0], sea.at[1], hsend.at[2], hrecv.at[2], (east, sub)),
        remote(ocean_ref, tile_in.at[0], hsend.at[3], hrecv.at[3], (east, sub)),
        remote(ocean_ref, tile_in.at[1], hsend.at[4], hrecv.at[4], (west, sub)),
        remote(edge.at[1], edge_in.at[2], hsend.at[7], hrecv.at[7], (mirror, sub)),
    ]
    for cp in ocean_copies:
        cp.start()
    to_north = remote(edge.at[1], edge_in.at[0], hsend.at[5], hrecv.at[5], (lon, north))
    to_south = remote(edge.at[0], edge_in.at[1], hsend.at[6], hrecv.at[6], (lon, south))

    @pl.when(sub < n_sub - 1)
    def _():
        to_north.start()

    @pl.when(sub > 0)
    def _():
        to_south.start()

    for cp in small[2:]:
        cp.wait()
    for g in range(groups):
        pair = jnp.concatenate([o2a_src_ref[g], o2a_wgt_ref[g]], axis=0)
        ids_a[g] = jnp.transpose(pair, (1, 0))
    ids_o[...] = jnp.zeros_like(ids_o)
    ids_o[:width, :orows] = a2o_src_ref[0]
    ids_o[width : 2 * width, :orows] = a2o_wgt_ref[0]
    ids_ocean = jnp.transpose(ids_o[...], (1, 0))[:orows]

    ocean_copies[0].wait()
    window = jnp.concatenate([sea[1], sea[0]], axis=0)
    band = pl.ds(sub * aband, aband)
    for g in range(groups):
        for k in range(width):
            src = ids_a[g, band, :][:, k : k + 1]
            tile = jnp.remainder(src % n_lon - lon + 1, n_lon)
            ids = tile * orows + (src // n_lon - sub * orows)
            picked[k, g * aband : (g + 1) * aband, :] = dot(one_hot(ids, 2 * orows), window)
    wg = jnp.concatenate([ids_a[g, band, :][:, width:] for g in range(groups)], axis=0)

    def sst_step(w, acc):
        part = jnp.where(wg[:, 0:1] == w, picked[0], 0.0)
        for k in range(1, width):
            part = part + jnp.where(wg[:, k : k + 1] == w, picked[k], 0.0)
        return acc + dot_nt(part, wbuf[w])

    acc = lax.fori_loop(
        0, nw, sst_step, jnp.zeros((groups * aband, LANES), jnp.float32), unroll=2
    )
    for g in range(groups):
        sst[:, g * LANES : (g + 1) * LANES] = acc[g * aband : (g + 1) * aband]

    sends2 = []
    for t in range(nchunk):
        for tt, cp in sends1:
            if tt == t:
                cp.wait()
        if t == 0:
            for cp in shares:
                cp.wait()
            for s in range(n_sub):

                def add_share(l, carry, s=s):
                    w = pltpu.roll(corr_in[s], lax.rem(LANES - l, LANES), 1)
                    e = pltpu.roll(corr_in[s], LANES - 1 - l - lev_dev, 1)
                    both = jnp.concatenate([w] * (groups - 1) + [e], axis=1)
                    ends = (wide == 0) | (wide == alon - 1)
                    old = cols[0, s * lev_dev + l]
                    cols[0, s * lev_dev + l] = old + jnp.where(ends, both, 0.0)
                    return carry

                lax.fori_loop(0, lev_dev, add_share, 0, unroll=4)

        def turn(i, carry, t=t):
            part = cols[t, pl.ds(i * ROWS, ROWS)]
            tmp[:, pl.ds(i * ROWS, ROWS), :] = jnp.swapaxes(part, 0, 1)
            return carry

        lax.fori_loop(0, levels // ROWS, turn, 0, unroll=2)

        def solve(r, carry, t=t):
            tmp2[r] = dot(inv[t * ROWS // rows_band], tmp[r])
            return carry

        lax.fori_loop(0, ROWS, solve, 0)

        def back(i, carry, t=t):
            part = tmp2[:, pl.ds(i * ROWS, ROWS), :]
            res[t, pl.ds(i * ROWS, ROWS)] = jnp.swapaxes(part, 0, 1)
            return carry

        lax.fori_loop(0, levels // ROWS, back, 0, unroll=2)
        for off in offs:
            peer = lax.rem(sub + off, n_sub)
            cp = remote(
                res.at[t, pl.ds(peer * lev_dev, lev_dev)],
                out_ref.at[:, pl.ds(sub * aband + t * ROWS, ROWS), :],
                send2.at[t, off],
                recv2.at[t, off],
                (lon, peer),
            )
            cp.start()
            sends2.append(cp)
        own = pltpu.make_async_copy(
            res.at[t, pl.ds(sub * lev_dev, lev_dev)],
            out_ref.at[:, pl.ds(sub * aband + t * ROWS, ROWS), :],
            own_sem.at[t],
        )
        own.start()
        sends2.append(own)

    fluxbuf[...] = heat_ref[...] * (sst[...] - res[:, levels - 1].reshape(aband, alon))
    flux_ref[...] = fluxbuf[...]
    fcopy = remote(fluxbuf, flux_in, hsend.at[8], hrecv.at[8], (west, sub))
    fcopy.start()
    for cp in ocean_copies[1:]:
        cp.wait()

    @pl.when(sub < n_sub - 1)
    def _():
        to_north.wait_send()
        to_south.wait_recv()

    @pl.when(sub > 0)
    def _():
        to_south.wait_send()
        to_north.wait_recv()

    fcopy.wait()

    blocks = jnp.concatenate(
        [fluxbuf[:, g * LANES : (g + 1) * LANES] for g in range(groups)]
        + [flux_in[:, g * LANES : (g + 1) * LANES] for g in range(groups)],
        axis=0,
    )
    for k in range(width):
        src = ids_ocean[:, k : k + 1]
        grp = jnp.remainder(src % ngroups - lon * groups, ngroups)
        ids = grp * aband + (src // ngroups - sub * aband)
        apicked[k] = dot(one_hot(ids, 2 * groups * aband), blocks)
    wa = ids_ocean[:, width:]

    def a2o_step(w, acc):
        part = jnp.where(wa[:, 0:1] == w, apicked[0], 0.0)
        for k in range(1, width):
            part = part + jnp.where(wa[:, k : k + 1] == w, apicked[k], 0.0)
        return acc + dot_nt(part, wbuf[w])

    flux_ocean = lax.fori_loop(
        0, nw, a2o_step, jnp.zeros((orows, LANES), jnp.float32), unroll=4
    )

    rev_r = lax.broadcasted_iota(jnp.int32, (LANES, LANES), 0)
    rev_c = lax.broadcasted_iota(jnp.int32, (LANES, LANES), 1)
    rev = jnp.where(rev_r + rev_c == LANES - 1, 1.0, 0.0).astype(jnp.float32)
    folded = dot(edge_in[2], rev)

    @pl.when(sub > 0)
    def _():
        edge[0] = edge_in[0]

    edge[1] = folded

    @pl.when(sub < n_sub - 1)
    def _():
        edge[1] = edge_in[1]

    olane = lax.broadcasted_iota(jnp.int32, (orows, LANES), 1)
    orow = lax.broadcasted_iota(jnp.int32, (orows, LANES), 0)
    diff = diff_ref[...]

    def step(l, carry):
        x = ocean_ref[l]
        ow = jnp.where(olane == 0, pltpu.roll(tile_in[0, l], 1, 1), pltpu.roll(x, 1, 1))
        oe = jnp.where(
            olane == LANES - 1,
            pltpu.roll(tile_in[1, l], LANES - 1, 1),
            pltpu.roll(x, LANES - 1, 1),
        )
        so = jnp.where(orow == 0, edge[0, pl.ds(l, 1), :], pltpu.roll(x, 1, 0))
        no = jnp.where(orow == orows - 1, edge[1, pl.ds(l, 1), :], pltpu.roll(x, orows - 1, 0))
        lap = ow + oe + no + so - 4.0 * x
        otmp[l] = maskf * (x + diff * lap)
        return carry

    lax.fori_loop(0, olev, step, 0, unroll=2)
    otmp[0] = otmp[0] + maskf * flux_ocean
    stepped = jnp.swapaxes(otmp[...], 0, 1)
    for r in range(orows):
        otmp2[r] = dot(oinv_ref[...], stepped[r])
    onew_ref[...] = jnp.swapaxes(otmp2[...], 0, 1)

    for cp in sends2:
        cp.wait()


def write_out(air, ocean, flux, air_out, ocean_out, flux_out, sem):
    step = air.shape[0] // WRITES
    copies = [
        pltpu.make_async_copy(
            air.at[pl.ds(i * step, step)], air_out.at[pl.ds(i * step, step)], sem.at[i]
        )
        for i in range(WRITES)
    ]
    copies.append(pltpu.make_async_copy(ocean, ocean_out, sem.at[WRITES]))
    copies.append(pltpu.make_async_copy(flux, flux_out, sem.at[WRITES + 1]))
    for cp in copies:
        cp.start()
    for cp in copies:
        cp.wait()


def per_device(
    atm_tracer,
    courant,
    column_inverse,
    heat_exchange_factor,
    ocean_temp,
    diffusivity,
    ocean_inverse,
    land_mask,
    regrid_weight_blocks,
    a2o_src,
    a2o_wgt,
    o2a_src,
    o2a_wgt,
):
    n_lon = lax.axis_size("lon")
    n_sub = lax.axis_size("sub")
    lev_dev, alat, alon = atm_tracer.shape
    levels = lev_dev * n_sub
    aband = alat // n_sub
    nchunk = aband // ROWS
    local_bands = column_inverse.shape[0] // n_sub
    olev, orows, olon = ocean_temp.shape
    groups = alon // LANES
    width = a2o_src.shape[2]
    f32 = jnp.float32
    vm = pl.BlockSpec(memory_space=pltpu.VMEM)
    hbm = pl.BlockSpec(memory_space=pltpu.HBM)
    anywhere = pl.BlockSpec(memory_space=pl.ANY)
    results = pl.pallas_call(
        functools.partial(kernel, n_lon, n_sub),
        out_shape=(
            pltpu.VMEM(atm_tracer.shape, f32),
            pltpu.VMEM(ocean_temp.shape, f32),
            pltpu.VMEM((aband, alon), f32),
        ),
        in_specs=[hbm] * 13,
        out_specs=(anywhere, vm, vm),
        scratch_shapes=[
            pltpu.VMEM((lev_dev, n_sub, aband, alon), f32),
            pltpu.VMEM((lev_dev, n_sub, aband, alon), f32),
            pltpu.VMEM((nchunk, n_sub, lev_dev, ROWS, alon), f32),
            pltpu.VMEM((nchunk, levels, ROWS, alon), f32),
            pltpu.VMEM((nchunk, levels, ROWS, alon), f32),
            pltpu.VMEM((ROWS, levels, alon), f32),
            pltpu.VMEM((ROWS, levels, alon), f32),
            pltpu.VMEM(regrid_weight_blocks.shape, f32),
            pltpu.VMEM((local_bands, levels, levels), f32),
            pltpu.VMEM((aband, alon), f32),
            pltpu.VMEM(ocean_temp.shape, f32),
            pltpu.VMEM(diffusivity.shape, f32),
            pltpu.VMEM(ocean_inverse.shape, f32),
            pltpu.VMEM(land_mask.shape, jnp.int32),
            pltpu.VMEM((1, width, orows), jnp.int32),
            pltpu.VMEM((1, width, orows), jnp.int32),
            pltpu.VMEM((groups, width, alat), jnp.int32),
            pltpu.VMEM((groups, width, alat), jnp.int32),
            pltpu.VMEM((groups, alat, 2 * width), jnp.int32),
            pltpu.VMEM((2 * width, LANES), jnp.int32),
            pltpu.VMEM((2, nchunk, n_sub, ROWS, LANES), f32),
            pltpu.VMEM((2, nchunk, n_sub, ROWS, LANES), f32),
            pltpu.VMEM((n_sub, ROWS, LANES), f32),
            pltpu.VMEM((n_sub, ROWS, LANES), f32),
            pltpu.VMEM((2, orows, olon), f32),
            pltpu.VMEM((2, olev, orows, olon), f32),
            pltpu.VMEM((2, olev, olon), f32),
            pltpu.VMEM((3, olev, olon), f32),
            pltpu.VMEM((aband, alon), f32),
            pltpu.VMEM((aband, alon), f32),
            pltpu.VMEM((width, groups * aband, LANES), f32),
            pltpu.VMEM((width, orows, LANES), f32),
            pltpu.VMEM((aband, alon), f32),
            pltpu.VMEM((olev, orows, olon), f32),
            pltpu.VMEM((orows, olev, olon), f32),
            pltpu.SemaphoreType.DMA((11,)),
            pltpu.SemaphoreType.DMA((2, nchunk)),
            pltpu.SemaphoreType.DMA((nchunk,)),
            pltpu.SemaphoreType.DMA((2, nchunk)),
            pltpu.SemaphoreType.DMA((2, nchunk)),
            pltpu.SemaphoreType.DMA((n_sub,)),
            pltpu.SemaphoreType.DMA((n_sub,)),
            pltpu.SemaphoreType.DMA((nchunk, n_sub)),
            pltpu.SemaphoreType.DMA((nchunk, n_sub)),
            pltpu.SemaphoreType.DMA((nchunk, n_sub)),
            pltpu.SemaphoreType.DMA((nchunk, n_sub)),
            pltpu.SemaphoreType.DMA((9,)),
            pltpu.SemaphoreType.DMA((9,)),
        ],
        compiler_params=pltpu.CompilerParams(
            collective_id=0, has_side_effects=True, vmem_limit_bytes=48 * 1024 * 1024
        ),
        name="step",
    )(*(pltpu.with_memory_space_constraint(v, pltpu.HBM) for v in (
        atm_tracer.reshape(lev_dev, n_sub, aband, alon),
        courant.reshape(lev_dev, n_sub, aband, alon),
        column_inverse,
        heat_exchange_factor,
        ocean_temp,
        diffusivity,
        ocean_inverse,
        land_mask,
        regrid_weight_blocks,
        jnp.transpose(a2o_src, (1, 2, 0)),
        jnp.transpose(a2o_wgt, (1, 2, 0)),
        jnp.transpose(o2a_src, (1, 2, 0)),
        jnp.transpose(o2a_wgt, (1, 2, 0)),
    )))
    return pl.pallas_call(
        write_out,
        out_shape=[jax.ShapeDtypeStruct(v.shape, f32) for v in results],
        in_specs=[anywhere] * 3,
        out_specs=[hbm] * 3,
        scratch_shapes=[pltpu.SemaphoreType.DMA((WRITES + 2,))],
        compiler_params=pltpu.CompilerParams(vmem_limit_bytes=1024 * 1024),
        name="write_out",
    )(*results)


def solution(mesh):
    return jax.shard_map(
        per_device,
        mesh=mesh,
        in_specs=(
            P("sub", None, "lon"),
            P("sub", None, "lon"),
            P(),
            P(None, "lon"),
            P(None, "sub", "lon"),
            P("sub", "lon"),
            P(),
            P("sub", "lon"),
            P(),
            P("sub", "lon", None),
            P("sub", "lon", None),
            P(None, "lon", None),
            P(None, "lon", None),
        ),
        out_specs=(P("sub", None, "lon"), P(None, "sub", "lon"), P("sub", "lon")),
        check_vma=False,
    )
```
